32 devices in a mesh: wide: 8 (over y, x, core), narrow: 4 (over z).
Axes of the slice: x: 2, y: 2, z: 4, core: 2. Of those that a mesh axis runs over, the one named last changes fastest.
Arguments:
- hidden: bfloat16 [1024, 4096], P('wide', 'narrow'), may hold values from -6 to 6
- head_weight: bfloat16 [32768, 4096], P('wide', 'narrow'), may hold values from -0.25 to 0.25
- lse: float32 [1024], replicated, may hold values from 12 to 14
- targets: int32 [1024], replicated, may hold values from 0 to 32767
- loss_weight: float32 [1024], replicated, may hold values from 16 to 48
- block_tiles: int32 [8, 8, 4], P(None, 'wide'), may hold values from 0 to 31, as said below
- block_counts: int32 [8, 8], P(None, 'wide'), may hold values from 0 to 4, as said below
- gate_pre: bfloat16 [1024, 7168], P('wide', 'narrow'), may hold values from -6 to 6
- up_pre: bfloat16 [1024, 7168], P('wide', 'narrow'), may hold values from -6 to 6
- down_weight: bfloat16 [7168, 4096], P('narrow'), may hold values from -0.0625 to 0.0625
Outputs:
- head_grad: bfloat16 [1024, 4096], P('wide', 'narrow')
- gate_grad: bfloat16 [1024, 7168], P('wide', 'narrow')
- up_grad: bfloat16 [1024, 7168], P('wide', 'narrow')
The draws below stay inside these ranges and needn't reach their ends.
Inputs may be any that keep to these rules, and one draw needn't show every extreme that they name: The first block_counts[b, s] entries of block_tiles[b, s] are distinct; the other entries are ignored. `block_counts`: some row block has 4 active tiles in some shard; one shard has exactly 16 active tiles over all row blocks, and no shard has more.
All inputs are finite; a program needn't handle non-finite values.
Results may differ from the reference program's by a relative error of at most 0.0035.
The reference program's roundings to bfloat16 on the way (of `cell_probs`) count: a program that leaves them out, or rounds other values in their place, can miss the bound.
Values may be sent and summed in bfloat16 or wider, within the bound.
No kernel may reach another device: no remote copies, remote signals or barrier semaphores. Data moves between devices by JAX's collectives and lax.ppermute only.
A program may use at most 128 MiB of HBM per device.

```python
import math
import jax
import jax.numpy as jnp
import numpy as np
from jax import lax

D = 4096
FF = 7168
VOC_DEV = 4096
TILE = 128
MAXT = 4
ROWS = 1024
SHARDS = 8
VOCAB = 32768
TILES_SHARD = 32
BLOCKS = 8


def tile_plan(key):
    planned = jax.random.fold_in(key, 4099)
    hot_key, rank_key, spare_key, tile_key = jax.random.split(planned, 4)
    hot_shard = jax.random.randint(hot_key, (), 0, SHARDS)
    ranking = jax.random.permutation(rank_key, BLOCKS)
    heavy_rows = jnp.where(ranking < BLOCKS // 2, MAXT, 0)
    spare = jax.random.randint(spare_key, (BLOCKS, SHARDS), 0, MAXT // 2 + 1)
    is_hot = jnp.arange(SHARDS) == hot_shard
    counts = jnp.where(is_hot[None, :], heavy_rows[:, None], spare).astype(jnp.int32)
    tile_keys = jax.random.split(tile_key, BLOCKS * SHARDS)
    chosen = jax.vmap(lambda one_key: jax.random.permutation(one_key, TILES_SHARD)[:MAXT])(tile_keys)
    return (counts, chosen.reshape(BLOCKS, SHARDS, MAXT).astype(jnp.int32))


def draw_block_counts(key, part):
    return tile_plan(key)[0]


def draw_block_tiles(key, part):
    return tile_plan(key)[1]


def draw_hidden(key, part):
    return jax.random.truncated_normal(key, -6.0, 6.0, (ROWS, D), jnp.float32).astype(jnp.bfloat16)


def plant(entries, key, low, high):
    index_at = [jax.random.randint(jax.random.fold_in(key, axis), (), 0, length) for axis, length in enumerate(entries.shape)]
    main_axis = entries.shape.index(max(entries.shape))
    neighbour = index_at[:main_axis] + [(index_at[main_axis] + 1) % entries.shape[main_axis]] + index_at[main_axis + 1:]
    return entries.at[tuple(index_at)].set(low).at[tuple(neighbour)].set(high)


def steps_of(key, extent, cuts, least, largest):
    level = 1.0
    for position, shards_of in cuts:
        steps = jax.random.uniform(jax.random.fold_in(jax.random.fold_in(key, 6), position), (shards_of,), jnp.float32, least / len(cuts), largest / len(cuts))
        level = level * jnp.repeat(jnp.exp(steps), extent[position] // shards_of).reshape((-1,) + (1,) * (len(extent) - 1 - position))
    return level


def cumulative_ranks(count, lean):
    loads = [(1 << 20) // math.isqrt(rank ** lean) + 1 for rank in range(1, count + 1)]
    deviation = 1 + sum(loads) // (1 << 30)
    return np.cumsum(np.array([max(1, weight // deviation) for weight in loads]))


def skewed_ids(own_key, dims, count, slope):
    table = cumulative_ranks(count, slope)
    pick = jax.random.randint(jax.random.fold_in(own_key, 1), dims, 0, int(table[count - 1]))
    standing = jnp.searchsorted(jnp.asarray(table, jnp.int32), pick, side="right")
    return jax.random.permutation(jax.random.fold_in(own_key, 2), count)[standing].astype(jnp.int32)


def noise(rng, extent, width, reach, cuts=(), kind=jnp.bfloat16):
    level = steps_of(rng, extent, cuts, -0.22, 0.18) if cuts else 1.0
    result = jax.random.normal(rng, extent, jnp.float32) * width * level
    return jnp.minimum(jnp.maximum(result, -reach), reach).astype(kind)


def setup_inputs(seed: int = 0) -> dict:
    streams_of = jax.random.split(jax.random.key(seed), 11)
    return {
        "hidden": draw_hidden(jax.random.fold_in(streams_of[10], 71), 0),
        "head_weight": noise(streams_of[1], (VOCAB, D), (D // 9) ** -0.5, 0.25, ((0, 8), (1, 4))),
        "lse": jnp.clip(jax.random.uniform(streams_of[2], (ROWS,), jnp.float32, 12.0, 14.0), 12.0, 14.0),
        "targets": plant(skewed_ids(streams_of[3], (ROWS,), VOCAB, 2), jax.random.fold_in(streams_of[3], 3), 0, VOCAB - 1).astype(jnp.int32),
        "loss_weight": jnp.clip(jax.random.uniform(streams_of[4], (ROWS,), jnp.float32, 16.0, 48.0), 16.0, 48.0),
        "block_tiles": draw_block_tiles(jax.random.fold_in(streams_of[10], 71), 0),
        "block_counts": draw_block_counts(jax.random.fold_in(streams_of[10], 71), 0),
        "gate_pre": noise(streams_of[7], (ROWS, FF), 1.5, 6.0, ((0, 8), (1, 4))),
        "up_pre": noise(streams_of[8], (ROWS, FF), 1.0, 6.0, ((0, 8), (1, 4))),
        "down_weight": noise(streams_of[9], (FF, D), FF ** -0.5, 0.0625, ((0, 4),)),
    }


def reference(hidden, head_weight, lse, targets, loss_weight, block_tiles, block_counts, gate_pre, up_pre, down_weight):
    blocks = ROWS // TILE
    shard_start = jnp.arange(SHARDS, dtype=jnp.int32)[:, None] * VOC_DEV
    within = jnp.arange(TILE, dtype=jnp.int32)
    slot_ids = jnp.arange(MAXT, dtype=jnp.int32)

    def one_block(items):
        row_block, lse_rows, scale_rows, tiles_row, counts_row, target_row = items
        first_cols = shard_start + tiles_row.astype(jnp.int32) * TILE
        columns = first_cols[:, :, None] + within[None, None, :]
        picked = jnp.take(head_weight, columns.reshape(-1).astype(jnp.int32), axis=0)
        picked = picked.astype(jnp.float32).reshape(SHARDS, MAXT, TILE, D)
        logits = jnp.einsum("rd,smcd->smrc", row_block.astype(jnp.float32), picked)
        scaled = jnp.exp(logits - lse_rows[None, None, :, None]) * scale_rows[None, None, :, None]
        live_slots = slot_ids[None, :] < counts_row[:, None]
        cell_probs = jnp.where(live_slots[:, :, None, None], scaled, jnp.zeros_like(scaled)).astype(jnp.bfloat16)
        cell_probs = lax.optimization_barrier(cell_probs).astype(jnp.float32)
        softmax_part = jnp.einsum("smrc,smcd->rd", cell_probs, picked)
        target_rows = jnp.take(head_weight, target_row.astype(jnp.int32), axis=0).astype(jnp.float32)
        return softmax_part - scale_rows[:, None] * target_rows

    grads = lax.map(one_block, (hidden.reshape(blocks, TILE, D), lse.reshape(blocks, TILE),
                                loss_weight.reshape(blocks, TILE), block_tiles, block_counts,
                                targets.reshape(blocks, TILE)))
    head_grad = grads.reshape(ROWS, D).astype(jnp.bfloat16)
    unit_grad = jnp.dot(head_grad, down_weight.T, preferred_element_type=jnp.float32)
    gate_value = gate_pre.astype(jnp.float32)
    up_value = up_pre.astype(jnp.float32)
    gate_sig = jax.nn.sigmoid(gate_value)
    up_grad = (unit_grad * gate_value * gate_sig).astype(jnp.bfloat16)
    gate_grad = (unit_grad * up_value * gate_sig * (1.0 + gate_value * (1.0 - gate_sig))).astype(jnp.bfloat16)
    return (head_grad, gate_grad, up_grad)
```

```python
import functools

import jax
import jax.numpy as jnp
from jax import lax
from jax.experimental import pallas as pl
from jax.experimental.pallas import tpu as pltpu
from jax.sharding import PartitionSpec as P

TILE = 128
PAD = 16
LEVELS = 32767.0
VMEM = pl.BlockSpec(memory_space=pltpu.VMEM)
SMEM = pl.BlockSpec(memory_space=pltpu.SMEM)
ANY = pl.BlockSpec(memory_space=pl.ANY)


def swap(x, axis, mask):
    if mask == 0:
        return x
    size = lax.axis_size(axis)
    return lax.ppermute(x, axis, [(i, i ^ mask) for i in range(size)])


def step_of(code):
    return jnp.exp2(code * 0.125) * (1.0 / LEVELS)


def encode(x):
    peak = jnp.max(jnp.abs(x), axis=0, keepdims=True)
    code = jnp.ceil(8.0 * jnp.log2(jnp.maximum(peak, 1e-30)) + 0.25)
    levels = jnp.round(x * (1.0 / step_of(code)))
    return levels.astype(jnp.int32).astype(jnp.int16), code.astype(jnp.int32)


def decode(levels, code):
    return levels.astype(jnp.int32).astype(jnp.float32) * step_of(code.astype(jnp.float32))


def slot_table(tiles_here, counts_here, slot_count):
    block_total, per_block = tiles_here.shape
    slot_live = (jnp.arange(per_block, dtype=jnp.int32)[None, :] < counts_here[:, None]).reshape(-1)
    before = jnp.arange(block_total * per_block, dtype=jnp.int32)
    position = (
        jnp.sum(jnp.where((before[:, None] >= before[None, :]) & slot_live[None, :], 1, 0), axis=1)
        - 1
    )
    select = (position[None, :] == jnp.arange(slot_count, dtype=jnp.int32)[:, None]) & slot_live[
        None, :
    ]
    chosen = select.astype(jnp.int32)
    block_ids = jnp.repeat(jnp.arange(block_total, dtype=jnp.int32), per_block)
    slot_blocks = jnp.sum(chosen * block_ids[None, :], axis=1)
    slot_tiles = jnp.sum(chosen * tiles_here.reshape(-1)[None, :], axis=1)
    return slot_blocks, slot_tiles, jnp.sum(slot_live.astype(jnp.int32)).reshape(1)


def logits_kernel(wide, narrow, slots, blocks_ref, tiles_ref, where_ref, *refs):
    parts, head = refs[:wide], refs[wide]
    own, sends = refs[wide + 1], refs[wide + 2 : wide + 1 + narrow]
    rows_v, tiles_v, row_sem, tile_sem = refs[wide + 1 + narrow :]
    me_w, me_n = where_ref[0], where_ref[1]
    per = slots // narrow
    row_copies = [
        pltpu.make_async_copy(parts[k], rows_v.at[k], row_sem.at[k]) for k in range(wide)
    ]
    for copy in row_copies:
        copy.start()
    order = [(k, i) for k in [*range(1, narrow), 0] for i in range(per)]

    def tile_copy(k, i):
        slot = (me_n ^ k) * per + i
        start = pl.multiple_of(tiles_ref[slot] * TILE, TILE)
        at = k * per + i
        return pltpu.make_async_copy(
            head.at[pl.ds(start, TILE), :], tiles_v.at[at], tile_sem.at[at]
        )

    for k, i in order:
        tile_copy(k, i).start()
    for copy in row_copies:
        copy.wait()
    for send in sends:
        send[per * TILE :, :] = jnp.zeros((send.shape[0] - per * TILE, TILE), jnp.int16)
    for k, i in order:
        tile_copy(k, i).wait()
        slot = (me_n ^ k) * per + i
        part = lax.dot_general(
            tiles_v[k * per + i],
            rows_v[blocks_ref[slot] ^ me_w],
            (((1,), (1,)), ((), ())),
            preferred_element_type=jnp.float32,
        )
        if k == 0:
            own[i * TILE : (i + 1) * TILE, :] = part
        else:
            levels, code = encode(part)
            sends[k - 1][i * TILE : (i + 1) * TILE, :] = levels
            sends[k - 1][per * TILE + i : per * TILE + i + 1, :] = code.astype(jnp.int16)


def probs_kernel(narrow, slots, blocks_ref, live_ref, where_ref, own, *refs):
    recvs, lse, weight, out = refs[: narrow - 1], refs[-3], refs[-2], refs[-1]
    per = slots // narrow
    codes = [recv[per * TILE :, :] for recv in recvs]
    for i in range(per):
        slot = where_ref[1] * per + i
        total = own[i * TILE : (i + 1) * TILE, :]
        for recv, code in zip(recvs, codes):
            total = total + decode(recv[i * TILE : (i + 1) * TILE, :], code[i : i + 1, :])
        block = blocks_ref[slot]
        scaled = jnp.exp(total - lse[pl.ds(block, 1), :]) * weight[pl.ds(block, 1), :]
        out[i * TILE : (i + 1) * TILE, :] = jnp.where(slot < live_ref[0], scaled, 0.0).astype(
            jnp.bfloat16
        )


def grads_kernel(
    wide, narrow, slots, parity, blocks_ref, tiles_ref, live_ref, where_ref, *refs
):
    probs, head, target_rows, factor, out = refs[:narrow], *refs[narrow : narrow + 4]
    tiles_v, target_v, tile_sem, target_sem = refs[narrow + 4 :]
    me_w, me_n = where_ref[0], where_ref[1]
    per = slots // narrow
    chips = wide // 2

    def target_copy(chip):
        block = me_w ^ (2 * chip + parity)
        start = pl.multiple_of(block * TILE, TILE)
        return pltpu.make_async_copy(
            target_rows.at[pl.ds(start, TILE), :], target_v.at[chip], target_sem.at[chip]
        )

    for chip in range(chips):
        target_copy(chip).start()

    def tile_copy(at, slot):
        start = pl.multiple_of(tiles_ref[slot] * TILE, TILE)
        return pltpu.make_async_copy(
            head.at[pl.ds(start, TILE), :], tiles_v.at[at], tile_sem.at[at]
        )

    def at_slot(k, i, act):
        slot = (me_n ^ k) * per + i
        owner = blocks_ref[slot] ^ me_w
        pl.when((slot < live_ref[0]) & ((owner & 1) == parity))(
            lambda: act(k * per + i, slot, owner)
        )

    for k in range(narrow):
        for i in range(per):
            at_slot(k, i, lambda at, slot, owner: tile_copy(at, slot).start())
    features = out.shape[1]
    for chip in range(chips):
        target_copy(chip).wait()
        block = me_w ^ (2 * chip + parity)
        weight = factor[pl.ds(pl.multiple_of(block * TILE, TILE), TILE), :]
        for lane in range(0, features, TILE):
            out[chip * TILE : (chip + 1) * TILE, lane : lane + TILE] = (
                -weight * target_v[chip, :, lane : lane + TILE].astype(jnp.float32)
            )
    for k in range(narrow):
        for i in range(per):

            def act(at, slot, owner, k=k, i=i):
                tile_copy(at, slot).wait()
                start = pl.multiple_of((owner >> 1) * TILE, TILE)
                out[pl.ds(start, TILE), :] += lax.dot_general(
                    probs[k][i * TILE : (i + 1) * TILE, :],
                    tiles_v[at],
                    (((0,), (0,)), ((), ())),
                    preferred_element_type=jnp.float32,
                )

            at_slot(k, i, act)


def pack_kernel(chips, mine, other, own, *refs):
    sends, (mine_v, other_v, mine_sem, other_sem) = refs[: chips - 1], refs[chips - 1 :]

    def copies(chip):
        rows = pl.ds(chip * TILE, TILE)
        return (
            pltpu.make_async_copy(mine.at[rows, :], mine_v.at[chip], mine_sem.at[chip]),
            pltpu.make_async_copy(other.at[rows, :], other_v.at[chip], other_sem.at[chip]),
        )

    order = [*range(1, chips), 0]
    for chip in order:
        for copy in copies(chip):
            copy.start()
    for chip in order:
        for copy in copies(chip):
            copy.wait()
        if chip == 0:
            own[...] = mine_v[chip] + other_v[chip]
            continue
        send = sends[chip - 1]
        for lane in range(0, own.shape[1], TILE):
            lanes = slice(lane, lane + TILE)
            levels, code = encode(mine_v[chip, :, lanes] + other_v[chip, :, lanes])
            send[:TILE, lanes] = levels
            send[TILE:, lanes] = jnp.broadcast_to(code, (PAD, TILE)).astype(jnp.int16)


def merge_kernel(own, *refs):
    recvs, out = refs[:-1], refs[-1]
    for lane in range(0, own.shape[1], TILE):
        lanes = slice(lane, lane + TILE)
        total = own[:, lanes]
        for recv in recvs:
            total = total + decode(recv[:TILE, lanes], recv[TILE : TILE + 1, lanes])
        out[:, lanes] = total.astype(jnp.bfloat16)


def unit_kernel(masks, has_sum, finish, chunk, where_ref, *refs):
    count = len(masks)
    pieces, down = refs[:count], refs[count]
    rest = refs[count + 1 :]
    if has_sum:
        summed, rest = rest[0], rest[1:]
    if finish:
        (gate, up, gate_out, up_out), rest = rest[:4], rest[4:]
        units = gate.shape[1]
    else:
        sum_out, rest = rest[0], rest[1:]
        units = sum_out.shape[1]
    down_v, sem = rest
    features = pieces[0].shape[1]
    steps = units // chunk

    def copy(step, at):
        start = pl.multiple_of((where_ref[1] ^ masks[at]) * features, features)
        rows = pl.ds(step * chunk, chunk)
        slot = step * count + at
        return pltpu.make_async_copy(
            down.at[rows, pl.ds(start, features)], down_v.at[slot], sem.at[slot]
        )

    for step in range(steps):
        for at in range(count):
            copy(step, at).start()
    for step in range(steps):
        lanes = slice(step * chunk, (step + 1) * chunk)
        total = summed[:, lanes] if has_sum else None
        for at in range(count):
            copy(step, at).wait()
            part = lax.dot_general(
                pieces[at][...],
                down_v[step * count + at],
                (((1,), (1,)), ((), ())),
                preferred_element_type=jnp.float32,
            )
            total = part if total is None else total + part
        if not finish:
            sum_out[:, lanes] = total
            continue
        g = gate[:, lanes].astype(jnp.float32)
        u = up[:, lanes].astype(jnp.float32)
        s = 1.0 / (1.0 + jnp.exp(-g))
        up_out[:, lanes] = (total * g * s).astype(jnp.bfloat16)
        gate_out[:, lanes] = (total * u * s * (1.0 + g * (1.0 - s))).astype(jnp.bfloat16)


def shape_of(shape, dtype):
    return jax.ShapeDtypeStruct(shape, dtype)


def params(mib):
    return pltpu.CompilerParams(vmem_limit_bytes=mib * 1024 * 1024)


def cost(flops, moved):
    return pl.CostEstimate(flops=flops, bytes_accessed=moved, transcendentals=0)


def on_device(
    hidden,
    head_weight,
    lse,
    targets,
    loss_weight,
    block_tiles,
    block_counts,
    gate_pre,
    up_pre,
    down_weight,
):
    f32, bf16, i16 = jnp.float32, jnp.bfloat16, jnp.int16
    row_count, features = hidden.shape
    vocab_here = head_weight.shape[0]
    wide, narrow = lax.axis_size("wide"), lax.axis_size("narrow")
    chips = wide // 2
    me_w, me_n = lax.axis_index("wide"), lax.axis_index("narrow")
    where = jnp.stack([me_w, me_n]).astype(jnp.int32)
    blocks, per_block = block_tiles.shape[0], block_tiles.shape[2]
    slots = blocks // 2 * per_block
    per = slots // narrow

    far = [swap(hidden, "wide", 2 * chip) for chip in range(chips)]
    near = [swap(part, "wide", 1) for part in far]
    parts = [part for pair in zip(far, near) for part in pair]

    slot_blocks, slot_tiles, live = slot_table(block_tiles[:, 0, :], block_counts[:, 0], slots)
    lse_blocks = lse.reshape(blocks, TILE)
    weight_blocks = loss_weight.reshape(blocks, TILE)
    local_ids = targets - me_w * vocab_here
    inside = (local_ids >= 0) & (local_ids < vocab_here)
    target_rows = jnp.take(head_weight, jnp.clip(local_ids, 0, vocab_here - 1), axis=0)
    factor = jnp.broadcast_to(
        jnp.where(inside, loss_weight, 0.0)[:, None], (blocks * TILE, TILE)
    )

    own, *sends = pl.pallas_call(
        functools.partial(logits_kernel, wide, narrow, slots),
        out_shape=[shape_of((per * TILE, TILE), f32)]
        + [shape_of((per * TILE + PAD, TILE), i16)] * (narrow - 1),
        in_specs=[SMEM] * 3 + [ANY] * (wide + 1),
        out_specs=[VMEM] * narrow,
        scratch_shapes=[
            pltpu.VMEM((wide, TILE, features), bf16),
            pltpu.VMEM((slots, TILE, features), bf16),
            pltpu.SemaphoreType.DMA((wide,)),
            pltpu.SemaphoreType.DMA((slots,)),
        ],
        compiler_params=params(40),
        cost_estimate=cost(2 * slots * TILE * TILE * features, slots * TILE * features * 2),
        name="logits",
    )(slot_blocks, slot_tiles, where, *parts, head_weight)
    recvs = [swap(send, "narrow", k + 1) for k, send in enumerate(sends)]
    probs = pl.pallas_call(
        functools.partial(probs_kernel, narrow, slots),
        out_shape=shape_of((per * TILE, TILE), bf16),
        in_specs=[SMEM] * 3 + [VMEM] * (narrow + 2),
        out_specs=VMEM,
        compiler_params=params(16),
        cost_estimate=cost(per * TILE * TILE * 20, per * TILE * TILE * 12),
        name="probs",
    )(slot_blocks, live, where, own, *recvs, lse_blocks, weight_blocks)
    all_probs = [swap(probs, "narrow", k) for k in range(narrow)]

    def grads(parity):
        return pl.pallas_call(
            functools.partial(grads_kernel, wide, narrow, slots, parity),
            out_shape=shape_of((chips * TILE, features), f32),
            in_specs=[SMEM] * 4 + [VMEM] * narrow + [ANY, ANY, VMEM],
            out_specs=VMEM,
            scratch_shapes=[
                pltpu.VMEM((slots, TILE, features), bf16),
                pltpu.VMEM((chips, TILE, features), bf16),
                pltpu.SemaphoreType.DMA((slots,)),
                pltpu.SemaphoreType.DMA((chips,)),
            ],
            compiler_params=params(40),
            cost_estimate=cost(slots * TILE * TILE * features, slots * TILE * features),
            name=f"grads_{parity}",
        )(slot_blocks, slot_tiles, live, where, *all_probs, head_weight, target_rows, factor)

    other = swap(grads(1), "wide", 1)
    mine = grads(0)
    kept, *packed = pl.pallas_call(
        functools.partial(pack_kernel, chips),
        out_shape=[shape_of((TILE, features), f32)]
        + [shape_of((TILE + PAD, features), i16)] * (chips - 1),
        in_specs=[ANY, ANY],
        out_specs=[VMEM] * chips,
        scratch_shapes=[
            pltpu.VMEM((chips, TILE, features), f32),
            pltpu.VMEM((chips, TILE, features), f32),
            pltpu.SemaphoreType.DMA((chips,)),
            pltpu.SemaphoreType.DMA((chips,)),
        ],
        compiler_params=params(40),
        cost_estimate=cost(chips * TILE * features * 8, chips * TILE * features * 10),
        name="pack",
    )(mine, other)
    arrived = [swap(part, "wide", 2 * (k + 1)) for k, part in enumerate(packed)]
    head_grad = pl.pallas_call(
        merge_kernel,
        out_shape=shape_of((TILE, features), bf16),
        in_specs=[VMEM] * chips,
        out_specs=VMEM,
        compiler_params=params(32),
        cost_estimate=cost(chips * TILE * features * 4, chips * TILE * features * 3),
        name="merge",
    )(kept, *arrived)

    pieces = [swap(head_grad, "narrow", k) for k in range(narrow)]
    units = gate_pre.shape[1]
    chunk = units // 2

    def unit(masks, summed, finish):
        count = len(masks)
        out = [shape_of((TILE, units), bf16)] * 2 if finish else shape_of((TILE, units), f32)
        extra = ([] if summed is None else [summed]) + ([gate_pre, up_pre] if finish else [])
        return pl.pallas_call(
            functools.partial(unit_kernel, masks, summed is not None, finish, chunk),
            out_shape=out,
            in_specs=[SMEM] + [VMEM] * count + [ANY] + [VMEM] * len(extra),
            out_specs=[VMEM] * 2 if finish else VMEM,
            scratch_shapes=[
                pltpu.VMEM((count * units // chunk, chunk, features), bf16),
                pltpu.SemaphoreType.DMA((count * units // chunk,)),
            ],
            compiler_params=params(40),
            cost_estimate=cost(2 * count * TILE * units * features, count * units * features * 2),
            name=f"unit_{masks[0]}",
        )(where, *[pieces[k] for k in masks], down_weight, *extra)

    summed = unit((0,), None, False)
    summed = unit((1,), summed, False)
    gate_grad, up_grad = unit(tuple(range(2, narrow)), summed, True)
    return head_grad, gate_grad, up_grad


def solution(mesh):
    in_specs = (
        P("wide", "narrow"),
        P("wide", "narrow"),
        P(),
        P(),
        P(),
        P(None, "wide", None),
        P(None, "wide"),
        P("wide", "narrow"),
        P("wide", "narrow"),
        P("narrow", None),
    )
    out_specs = (P("wide", "narrow"), P("wide", "narrow"), P("wide", "narrow"))
    return jax.shard_map(
        on_device, mesh=mesh, in_specs=in_specs, out_specs=out_specs, check_vma=False
    )
```

```python
import functools
import math

import jax
import jax.numpy as jnp
from jax import lax
from jax.experimental import pallas as pl
from jax.experimental.pallas import tpu as pltpu
from jax.sharding import PartitionSpec as P

TILE = 128
PAD = 16
GROUPS = 2
HALVES = 2
LARGE = 50
LEVELS = 32767.0
VMEM = pl.BlockSpec(memory_space=pltpu.VMEM)
SMEM = pl.BlockSpec(memory_space=pltpu.SMEM)
ANY = pl.BlockSpec(memory_space=pl.ANY)
HBM = pl.BlockSpec(memory_space=pltpu.HBM)


def swap(x, axis, mask):
    if mask == 0:
        return x
    size = lax.axis_size(axis)
    return lax.ppermute(x, axis, [(i, i ^ mask) for i in range(size)])


def step_of(code):
    return jnp.exp2(code * 0.125) * (1.0 / LEVELS)


def encode(x):
    peak = jnp.max(jnp.abs(x), axis=0, keepdims=True)
    code = jnp.ceil(8.0 * jnp.log2(jnp.maximum(peak, 1e-30)) + 0.25)
    levels = jnp.round(x * (1.0 / step_of(code)))
    return levels.astype(jnp.int32).astype(jnp.int16), code.astype(jnp.int32)


def decode(levels, code):
    return levels.astype(jnp.int32).astype(jnp.float32) * step_of(code.astype(jnp.float32))


def slot_table(tiles_here, counts_here, slot_count):
    block_total, per_block = tiles_here.shape
    slot_live = (jnp.arange(per_block, dtype=jnp.int32)[None, :] < counts_here[:, None]).reshape(-1)
    before = jnp.arange(block_total * per_block, dtype=jnp.int32)
    position = (
        jnp.sum(jnp.where((before[:, None] >= before[None, :]) & slot_live[None, :], 1, 0), axis=1)
        - 1
    )
    select = (position[None, :] == jnp.arange(slot_count, dtype=jnp.int32)[:, None]) & slot_live[
        None, :
    ]
    chosen = select.astype(jnp.int32)
    block_ids = jnp.repeat(jnp.arange(block_total, dtype=jnp.int32), per_block)
    slot_blocks = jnp.sum(chosen * block_ids[None, :], axis=1)
    slot_tiles = jnp.sum(chosen * tiles_here.reshape(-1)[None, :], axis=1)
    return slot_blocks, slot_tiles, jnp.sum(slot_live.astype(jnp.int32)).reshape(1)


def logits_kernel(wide, narrow, slots, group, blocks_ref, tiles_ref, where_ref, head, *refs):
    me_w, me_n = where_ref[0], where_ref[1]
    per = slots // narrow
    share = per // GROUPS
    *refs, tiles, tile_sem = refs
    order = [(k, i) for k in [*range(1, narrow), 0] for i in range(share)]

    def slot_of(k, i):
        return (me_n ^ k) * per + group * share + i

    def fetch(k, i):
        start = pl.multiple_of(tiles_ref[slot_of(k, i)] * TILE, TILE)
        at = k * share + i
        return pltpu.make_async_copy(head.at[pl.ds(start, TILE), :], tiles.at[at], tile_sem.at[at])

    for k, i in order:
        fetch(k, i).start()
    if group == 0:
        parts, own, sends = refs[:wide], refs[wide], refs[wide + 1 : wide + narrow]
        rows_all, sem = refs[wide + narrow :]
        copies = [
            pltpu.make_async_copy(parts[k], rows_all.at[pl.ds(k * TILE, TILE), :], sem.at[k])
            for k in range(wide)
        ]
        for copy in copies:
            copy.start()
        for copy in copies:
            copy.wait()
    else:
        rows_all, own, sends = refs[0], refs[1], refs[2:]
    for send in sends:
        send[share * TILE :, :] = jnp.zeros((send.shape[0] - share * TILE, TILE), jnp.int16)
    for k, i in order:
        start = pl.multiple_of((blocks_ref[slot_of(k, i)] ^ me_w) * TILE, TILE)
        fetch(k, i).wait()
        part = lax.dot_general(
            rows_all[pl.ds(start, TILE), :],
            tiles[k * share + i],
            (((1,), (1,)), ((), ())),
            preferred_element_type=jnp.float32,
        )
        if k == 0:
            own[i * TILE : (i + 1) * TILE, :] = part
        else:
            levels, code = encode(part)
            sends[k - 1][i * TILE : (i + 1) * TILE, :] = levels
            sends[k - 1][share * TILE + i : share * TILE + i + 1, :] = code.astype(jnp.int16)


def probs_kernel(narrow, slots, group, blocks_ref, live_ref, where_ref, own, *refs):
    recvs, lse, weight, out = refs[: narrow - 1], refs[-3], refs[-2], refs[-1]
    per = slots // narrow
    share = per // GROUPS
    codes = [recv[share * TILE :, :] for recv in recvs]
    for i in range(share):
        slot = where_ref[1] * per + group * share + i
        total = own[i * TILE : (i + 1) * TILE, :]
        for recv, code in zip(recvs, codes):
            total = total + decode(recv[i * TILE : (i + 1) * TILE, :], code[i : i + 1, :])
        rows = pl.ds(pl.multiple_of(blocks_ref[slot] * TILE, TILE), TILE)
        scaled = jnp.exp(total - lse[rows, :]) * weight[rows, :]
        out[i * TILE : (i + 1) * TILE, :] = jnp.where(slot < live_ref[0], scaled, 0.0).astype(
            jnp.bfloat16
        )


def grads_kernel(wide, narrow, slots, half, blocks_ref, tiles_ref, where_ref, head, *refs):
    probs = refs[: narrow * GROUPS]
    first_rows, last_rows, factor, mine, other, total, tiles, sem = refs[narrow * GROUPS :]
    me_w, me_n = where_ref[0], where_ref[1]
    per = slots // narrow
    share = per // GROUPS
    width = mine.shape[1]

    def fetch(slot):
        start = pl.multiple_of(tiles_ref[slot] * TILE, TILE)
        part = head.at[pl.ds(start, TILE), pl.ds(half * width, width)]
        return pltpu.make_async_copy(part, tiles.at[slot], sem.at[slot])

    for slot in range(slots):
        fetch(slot).start()
    blocks = factor.shape[0] // TILE
    for block in range(blocks):
        source = first_rows if block < blocks // 2 else last_rows
        start = (block % (blocks // 2)) * TILE
        weight = -factor[block * TILE : (block + 1) * TILE, :]
        for lane in range(0, width, TILE):
            at = half * width + lane
            total[block ^ me_w, :, lane : lane + TILE] = weight * source[
                start : start + TILE, at : at + TILE
            ].astype(jnp.float32)
    for slot in range(slots):
        fetch(slot).wait()
    for k in range(narrow):
        for group in range(GROUPS):
            for i in range(share):
                slot = (me_n ^ k) * per + group * share + i
                total[blocks_ref[slot] ^ me_w] += jnp.dot(
                    probs[k * GROUPS + group][i * TILE : (i + 1) * TILE, :],
                    tiles[slot],
                    preferred_element_type=jnp.float32,
                )
    for chip in range(wide // 2):
        mine[chip * TILE : (chip + 1) * TILE, :] = total[2 * chip]
        other[chip * TILE : (chip + 1) * TILE, :] = total[2 * chip + 1]


def pack_kernel(chips, mine, other, own, *sends):
    for chip in [*range(1, chips), 0]:
        rows = slice(chip * TILE, (chip + 1) * TILE)
        if chip == 0:
            own[...] = mine[rows, :] + other[rows, :]
            continue
        send = sends[chip - 1]
        for lane in range(0, own.shape[1], TILE):
            lanes = slice(lane, lane + TILE)
            levels, code = encode(mine[rows, lanes] + other[rows, lanes])
            send[:TILE, lanes] = levels
            send[TILE:, lanes] = jnp.broadcast_to(code, (PAD, TILE)).astype(jnp.int16)


def merge_kernel(own, *refs):
    recvs, out = refs[:-1], refs[-1]
    for lane in range(0, own.shape[1], TILE):
        lanes = slice(lane, lane + TILE)
        total = own[:, lanes]
        for recv in recvs:
            total = total + decode(recv[:TILE, lanes], recv[TILE : TILE + 1, lanes])
        out[:, lanes] = total.astype(jnp.bfloat16)


def unit_kernel(keys, kind, chunk, where_ref, *refs):
    count = len(keys)
    pieces, down = refs[:count], refs[count]
    rest = refs[count + 1 :]
    if kind != "first":
        summed, rest = rest[0], rest[1:]
    if kind == "last":
        (gate, up, gate_out, up_out), rest = rest[:4], rest[4:]
        units = gate.shape[1]
    else:
        sum_out, rest = rest[0], rest[1:]
        units = sum_out.shape[1]
    if kind == "first":
        grad_out, rest = rest[0], rest[1:]
        width = pieces[0].shape[1]
        for at in range(count):
            grad_out[:, at * width : (at + 1) * width] = pieces[at][...]
    down_v, sem = rest
    width = pieces[0].shape[1]
    steps = units // chunk

    def copy(step, at):
        mask, half = keys[at]
        start = pl.multiple_of((where_ref[1] ^ mask) * (width * HALVES) + half * width, width)
        rows = pl.ds(step * chunk, chunk)
        slot = step * count + at
        return pltpu.make_async_copy(
            down.at[rows, pl.ds(start, width)], down_v.at[slot], sem.at[slot]
        )

    for step in range(steps):
        for at in range(count):
            copy(step, at).start()
    for step in range(steps):
        lanes = slice(step * chunk, (step + 1) * chunk)
        total = None if kind == "first" else summed[:, lanes]
        for at in range(count):
            copy(step, at).wait()
            part = lax.dot_general(
                pieces[at][...],
                down_v[step * count + at],
                (((1,), (1,)), ((), ())),
                preferred_element_type=jnp.float32,
            )
            total = part if total is None else total + part
        if kind != "last":
            sum_out[:, lanes] = total
            continue
        g = gate[:, lanes].astype(jnp.float32)
        u = up[:, lanes].astype(jnp.float32)
        s = 1.0 / (1.0 + jnp.exp(-g))
        up_out[:, lanes] = (total * g * s).astype(jnp.bfloat16)
        gate_out[:, lanes] = (total * u * s * (1.0 + g * (1.0 - s))).astype(jnp.bfloat16)


def shape_of(shape, dtype):
    return jax.ShapeDtypeStruct(shape, dtype)


def call(kernel, name, outs, ins, args, flops, moved, scratch=(), mib=16):
    return pl.pallas_call(
        kernel,
        out_shape=outs,
        in_specs=ins,
        out_specs=[VMEM] * len(outs),
        scratch_shapes=list(scratch),
        compiler_params=pltpu.CompilerParams(vmem_limit_bytes=mib * 1024 * 1024),
        cost_estimate=pl.CostEstimate(flops=flops, bytes_accessed=moved, transcendentals=0),
        name=name,
    )(*args)


def on_device(
    hidden,
    head_weight,
    lse,
    targets,
    loss_weight,
    block_tiles,
    block_counts,
    gate_pre,
    up_pre,
    down_weight,
):
    f32, bf16, i16 = jnp.float32, jnp.bfloat16, jnp.int16
    row_count, features = hidden.shape
    vocab_here = head_weight.shape[0]
    wide, narrow = lax.axis_size("wide"), lax.axis_size("narrow")
    chips = wide // 2
    me_w, me_n = lax.axis_index("wide"), lax.axis_index("narrow")
    where = jnp.stack([me_w, me_n]).astype(jnp.int32)
    blocks, per_block = block_tiles.shape[0], block_tiles.shape[2]
    slots = blocks // 2 * per_block
    share = slots // narrow // GROUPS
    width = features // HALVES
    rows_all = blocks * TILE

    far = [swap(hidden, "wide", 2 * chip) for chip in range(chips)]

    slot_blocks, slot_tiles, live = slot_table(block_tiles[:, 0, :], block_counts[:, 0], slots)
    local_ids = targets - me_w * vocab_here
    inside = (local_ids >= 0) & (local_ids < vocab_here)
    clipped = jnp.clip(local_ids, 0, vocab_here - 1)

    def over_lanes(x):
        return jnp.broadcast_to(x[:, None], (rows_all, TILE))

    first_rows = jnp.take(head_weight, clipped[: rows_all // 2], axis=0)
    far[1], first_rows = lax.optimization_barrier((far[1], first_rows))
    near = [swap(part, "wide", 1) for part in far]
    parts = [part for pair in zip(far, near) for part in pair]
    lse_rows, weight_rows = over_lanes(lse), over_lanes(loss_weight)
    factor = over_lanes(jnp.where(inside, loss_weight, 0.0))

    probs = []
    gathered = None
    for group in range(GROUPS):
        outs = [shape_of((share * TILE, TILE), f32)]
        outs += [shape_of((share * TILE + PAD, TILE), i16)] * (narrow - 1)
        first = group == 0
        flops = 2 * slots * TILE * TILE * features // GROUPS
        result = call(
            functools.partial(logits_kernel, wide, narrow, slots, group),
            f"logits_{group}",
            outs + [shape_of((rows_all, features), bf16)] * first,
            [SMEM] * 3 + [HBM] + ([ANY] * wide if first else [VMEM]),
            (slot_blocks, slot_tiles, where, head_weight, *(parts if first else [gathered])),
            flops,
            slots * TILE * features,
            [pltpu.SemaphoreType.DMA((wide,))] * first
            + [
                pltpu.VMEM((slots // GROUPS, TILE, features), bf16),
                pltpu.SemaphoreType.DMA((slots // GROUPS,)),
            ],
            LARGE,
        )
        if first:
            *result, gathered = result
        own, *sends = result
        recvs = [swap(send, "narrow", k + 1) for k, send in enumerate(sends)]
        (prob,) = call(
            functools.partial(probs_kernel, narrow, slots, group),
            f"probs_{group}",
            [shape_of((share * TILE, TILE), bf16)],
            [SMEM] * 3 + [VMEM] * (narrow + 2),
            (slot_blocks, live, where, own, *recvs, lse_rows, weight_rows),
            share * TILE * TILE * 20,
            share * TILE * TILE * 12,
        )
        if not first:
            prob, clipped = lax.optimization_barrier((prob, clipped))
        probs.append([swap(prob, "narrow", k) for k in range(narrow)])
    last_rows = jnp.take(head_weight, clipped[rows_all // 2 :], axis=0)
    all_probs = [probs[group][k] for k in range(narrow) for group in range(GROUPS)]

    halves = []
    for half in range(HALVES):
        mine, other = call(
            functools.partial(grads_kernel, wide, narrow, slots, half),
            f"grads_{half}",
            [shape_of((chips * TILE, width), f32)] * 2,
            [SMEM] * 3 + [HBM] + [VMEM] * (narrow * GROUPS + 3),
            (
                *(slot_blocks, slot_tiles, where, head_weight),
                *(*all_probs, first_rows, last_rows, factor),
            ),
            2 * slots * TILE * TILE * width,
            slots * TILE * width * 4,
            [
                pltpu.VMEM((wide, TILE, width), f32),
                pltpu.VMEM((slots, TILE, width), bf16),
                pltpu.SemaphoreType.DMA((slots,)),
            ],
            LARGE,
        )
        halves.append((mine, swap(other, "wide", 1)))
    grads = []
    for half, (mine, other) in enumerate(halves):
        kept, *packed = call(
            functools.partial(pack_kernel, chips),
            f"pack_{half}",
            [shape_of((TILE, width), f32)]
            + [shape_of((TILE + PAD, width), i16)] * (chips - 1),
            [VMEM] * 2,
            (mine, other),
            chips * TILE * width * 8,
            chips * TILE * width * 10,
        )
        arrived = [swap(part, "wide", 2 * (k + 1)) for k, part in enumerate(packed)]
        (grad,) = call(
            merge_kernel,
            f"merge_{half}",
            [shape_of((TILE, width), bf16)],
            [VMEM] * chips,
            (kept, *arrived),
            chips * TILE * width * 4,
            chips * TILE * width * 3,
        )
        grads.append(grad)

    pieces = {
        (k, half): swap(grad, "narrow", k) for half, grad in enumerate(grads) for k in range(narrow)
    }
    units = gate_pre.shape[1]
    chunk = math.gcd(units, 256)

    def unit(keys, kind, *extra):
        count = len(keys)
        outs = [shape_of((TILE, units), f32)]
        if kind == "first":
            outs.append(shape_of((TILE, features), bf16))
        if kind == "last":
            outs = [shape_of((TILE, units), bf16)] * 2
        return call(
            functools.partial(unit_kernel, keys, kind, chunk),
            f"unit_{keys[0][0]}_{keys[0][1]}",
            outs,
            [SMEM] + [VMEM] * count + [HBM] + [VMEM] * len(extra),
            (where, *[pieces[key] for key in keys], down_weight, *extra),
            2 * count * TILE * units * width,
            count * units * width * 2,
            [
                pltpu.VMEM((count * units // chunk, chunk, width), bf16),
                pltpu.SemaphoreType.DMA((count * units // chunk,)),
            ],
            LARGE,
        )

    summed, head_grad = unit([(0, half) for half in range(HALVES)], "first")
    (summed,) = unit([(k, 0) for k in range(1, narrow)], "more", summed)
    (summed,) = unit([(1, 1)], "more", summed)
    gate_grad, up_grad = unit(
        [(k, 1) for k in range(2, narrow)], "last", summed, gate_pre, up_pre
    )
    return head_grad, gate_grad, up_grad


def solution(mesh):
    in_specs = (
        P("wide", "narrow"),
        P("wide", "narrow"),
        P(),
        P(),
        P(),
        P(None, "wide", None),
        P(None, "wide"),
        P("wide", "narrow"),
        P("wide", "narrow"),
        P("narrow", None),
    )
    out_specs = (P("wide", "narrow"), P("wide", "narrow"), P("wide", "narrow"))
    return jax.shard_map(
        on_device, mesh=mesh, in_specs=in_specs, out_specs=out_specs, check_vma=False
    )
```

```python
import functools

import jax
import jax.numpy as jnp
from jax import lax
from jax.experimental import pallas as pl
from jax.experimental.pallas import tpu as pltpu
from jax.sharding import PartitionSpec as P


TILE = 128
PAD = 8
GROUPS = 2
HALVES = 2
LARGE = 50
MEDIUM = 46
LEVELS = 32767.0
VMEM = pl.BlockSpec(memory_space=pltpu.VMEM)
SMEM = pl.BlockSpec(memory_space=pltpu.SMEM)
ANY = pl.BlockSpec(memory_space=pl.ANY)
HBM = pl.BlockSpec(memory_space=pltpu.HBM)


def swap(x, axis, mask):
    if mask == 0:
        return x
    size = lax.axis_size(axis)
    return lax.ppermute(x, axis, [(i, i ^ mask) for i in range(size)])


def step_of(code):
    return jnp.exp2(code * 0.125) * (1.0 / LEVELS)


def encode(x):
    peak = jnp.max(jnp.abs(x), axis=0, keepdims=True)
    code = jnp.ceil(8.0 * jnp.log2(jnp.maximum(peak, 1e-30)) + 0.25)
    levels = jnp.round(x * (1.0 / step_of(code)))
    return levels.astype(jnp.int32).astype(jnp.int16), code.astype(jnp.int32)


def decode(levels, code):
    return levels.astype(jnp.int32).astype(jnp.float32) * step_of(code.astype(jnp.float32))


def slots_kernel(slots, tiles_ref, counts_ref, blocks_out, tiles_out, live_out):
    blocks, _, per_block = tiles_ref.shape
    for slot in range(slots):
        blocks_out[slot] = 0
        tiles_out[slot] = 0
    live = jnp.int32(0)
    for block in range(blocks):
        count = counts_ref[block, 0]
        for j in range(per_block):

            @pl.when(j < count)
            def _(block=block, j=j, slot=live + j):
                blocks_out[slot] = block
                tiles_out[slot] = tiles_ref[block, 0, j]

        live = live + count
    live_out[0] = live


def logits_kernel(wide, narrow, slots, group, blocks_ref, tiles_ref, where_ref, head, *refs):
    me_w, me_n = where_ref[0], where_ref[1]
    per = slots // narrow
    share = per // GROUPS
    parts, own, sends = refs[:wide], refs[wide], refs[wide + 1 : wide + narrow]
    tiles, rows, row_sem, tile_sem = refs[wide + narrow :]
    order = [(k, i) for k in [*range(1, narrow), 0] for i in range(share)]

    def slot_of(k, i):
        return (me_n ^ k) * per + group * share + i

    def fetch(k, i):
        at = k * share + i
        start = pl.multiple_of(tiles_ref[slot_of(k, i)] * TILE, TILE)
        return pltpu.make_async_copy(
            head.at[pl.ds(start, TILE), :], tiles.at[pl.ds(at * TILE, TILE), :], tile_sem.at[at]
        )

    for k, i in order:
        fetch(k, i).start()
    copies = [pltpu.make_async_copy(parts[k], rows.at[k], row_sem.at[k]) for k in range(wide)]
    for copy in copies:
        copy.start()
    for send in sends:
        send[share * TILE :, :] = jnp.zeros((send.shape[0] - share * TILE, TILE), jnp.int16)
    for copy in copies:
        copy.wait()
    for k, i in order:
        at = k * share + i
        fetch(k, i).wait()
        part = lax.dot_general(
            rows[blocks_ref[slot_of(k, i)] ^ me_w],
            tiles[at * TILE : (at + 1) * TILE, :],
            (((1,), (1,)), ((), ())),
            preferred_element_type=jnp.float32,
        )
        if k == 0:
            own[i * TILE : (i + 1) * TILE, :] = part
        else:
            levels, code = encode(part)
            sends[k - 1][i * TILE : (i + 1) * TILE, :] = levels
            sends[k - 1][share * TILE + i : share * TILE + i + 1, :] = code.astype(jnp.int16)


def probs_kernel(narrow, slots, group, blocks_ref, live_ref, where_ref, own, *refs):
    recvs, lse, weight, out = refs[: narrow - 1], refs[-3], refs[-2], refs[-1]
    per = slots // narrow
    share = per // GROUPS
    codes = [recv[share * TILE :, :] for recv in recvs]
    for i in range(share):
        slot = where_ref[1] * per + group * share + i
        total = own[i * TILE : (i + 1) * TILE, :]
        for recv, code in zip(recvs, codes):
            total = total + decode(recv[i * TILE : (i + 1) * TILE, :], code[i : i + 1, :])
        rows = pl.ds(pl.multiple_of(blocks_ref[slot] * TILE, TILE), TILE)
        scaled = jnp.exp(total - lse[rows, :]) * weight[rows, :]
        out[i * TILE : (i + 1) * TILE, :] = jnp.where(slot < live_ref[0], scaled, 0.0).astype(
            jnp.bfloat16
        )


def grads_kernel(wide, narrow, slots, half, blocks_ref, where_ref, *refs):
    probs = refs[: narrow * GROUPS]
    tiles = refs[narrow * GROUPS : narrow * GROUPS + GROUPS]
    target_rows, factor, mine, other, total = refs[narrow * GROUPS + GROUPS :]
    me_w, me_n = where_ref[0], where_ref[1]
    per = slots // narrow
    share = per // GROUPS
    width = mine.shape[1]
    for block in range(factor.shape[0] // TILE):
        rows = slice(block * TILE, (block + 1) * TILE)
        weight = -factor[rows, :]
        for lane in range(0, width, TILE):
            at = half * width + lane
            total[block ^ me_w, :, lane : lane + TILE] = weight * target_rows[
                rows, at : at + TILE
            ].astype(jnp.float32)
    for k in range(narrow):
        for group in range(GROUPS):
            for i in range(share):
                slot = (me_n ^ k) * per + group * share + i
                total[blocks_ref[slot] ^ me_w] += jnp.dot(
                    probs[k * GROUPS + group][i * TILE : (i + 1) * TILE, :],
                    tiles[group][
                        (k * share + i) * TILE : (k * share + i + 1) * TILE,
                        half * width : (half + 1) * width,
                    ],
                    preferred_element_type=jnp.float32,
                )
    for chip in range(wide // 2):
        mine[chip * TILE : (chip + 1) * TILE, :] = total[2 * chip]
        other[chip * TILE : (chip + 1) * TILE, :] = total[2 * chip + 1]


def pack_kernel(chips, mine, other, own, *sends):
    for chip in [*range(1, chips), 0]:
        rows = slice(chip * TILE, (chip + 1) * TILE)
        if chip == 0:
            own[...] = mine[rows, :] + other[rows, :]
            continue
        send = sends[chip - 1]
        for lane in range(0, own.shape[1], TILE):
            lanes = slice(lane, lane + TILE)
            levels, code = encode(mine[rows, lanes] + other[rows, lanes])
            send[:TILE, lanes] = levels
            send[TILE:, lanes] = jnp.broadcast_to(code, (PAD, TILE)).astype(jnp.int16)


def merge_kernel(own, *refs):
    recvs, out = refs[:-1], refs[-1]
    for lane in range(0, own.shape[1], TILE):
        lanes = slice(lane, lane + TILE)
        total = own[:, lanes]
        for recv in recvs:
            total = total + decode(recv[:TILE, lanes], recv[TILE : TILE + 1, lanes])
        out[:, lanes] = total.astype(jnp.bfloat16)


def down_copies(keys, where_ref, down, out, sem, rows):
    width = out.shape[-1]

    def copy(at):
        mask, half = keys[at]
        start = pl.multiple_of((where_ref[1] ^ mask) * (width * HALVES) + half * width, width)
        return pltpu.make_async_copy(down.at[rows, pl.ds(start, width)], out.at[at], sem.at[at])

    return [copy(at) for at in range(len(keys))]


def hold_kernel(keys, where_ref, down, out, sem):
    copies = down_copies(keys, where_ref, down, out, sem, slice(None))
    for copy in copies:
        copy.start()
    for copy in copies:
        copy.wait()


def unit_kernel(keys, splits, kind, chunk, where_ref, *refs):
    count, inputs = len(keys), sum(splits)
    arrived, down, refs = list(refs[:inputs]), refs[inputs], refs[inputs + 1 :]
    units = down.shape[-2]
    width = arrived[0].shape[1]
    pieces = []
    for split in splits:
        piece = arrived.pop(0)[...]
        for _ in range(split - 1):
            piece = piece + arrived.pop(0)[...]
        pieces.append(piece)
    if kind == "last":
        summed, gate, up, gate_out, up_out = refs
    else:
        *refs, down_v, sem = refs
        if kind == "first":
            sum_out, grad_out = refs
            for at in range(count):
                grad_out[:, at * width : (at + 1) * width] = pieces[at]
        else:
            summed, sum_out = refs
    steps = [pl.ds(at, chunk) for at in range(0, units, chunk)]
    if kind != "last":
        copies = [
            down_copies(keys, where_ref, down, down_v.at[step], sem.at[step], rows)
            for step, rows in enumerate(steps)
        ]
        for copy in sum(copies, []):
            copy.start()
    for step, rows in enumerate(steps):
        total = None if kind == "first" else summed[:, rows]
        for at in range(count):
            if kind != "last":
                copies[step][at].wait()
            part = lax.dot_general(
                pieces[at],
                down[at, rows, :] if kind == "last" else down_v[step, at],
                (((1,), (1,)), ((), ())),
                preferred_element_type=jnp.float32,
            )
            total = part if total is None else total + part
        if kind != "last":
            sum_out[:, rows] = total
            continue
        g = gate[:, rows].astype(jnp.float32)
        u = up[:, rows].astype(jnp.float32)
        s = 1.0 / (1.0 + jnp.exp(-g))
        up_out[:, rows] = (total * g * s).astype(jnp.bfloat16)
        gate_out[:, rows] = (total * u * s * (1.0 + g * (1.0 - s))).astype(jnp.bfloat16)


def shape_of(shape, dtype):
    return jax.ShapeDtypeStruct(shape, dtype)


def call(kernel, outs, ins, args, flops, moved, scratch=(), mib=16, scalars=0):
    return pl.pallas_call(
        kernel,
        out_shape=outs,
        in_specs=ins,
        out_specs=[SMEM] * scalars + [VMEM] * (len(outs) - scalars),
        scratch_shapes=list(scratch),
        compiler_params=pltpu.CompilerParams(vmem_limit_bytes=mib * 1024 * 1024),
        cost_estimate=pl.CostEstimate(flops=flops, bytes_accessed=moved, transcendentals=0),
    )(*args)


def on_device(
    hidden,
    head_weight,
    lse,
    targets,
    loss_weight,
    block_tiles,
    block_counts,
    gate_pre,
    up_pre,
    down_weight,
):
    f32, bf16, i16 = jnp.float32, jnp.bfloat16, jnp.int16
    _, features = hidden.shape
    vocab_here = head_weight.shape[0]
    wide, narrow = lax.axis_size("wide"), lax.axis_size("narrow")
    chips = wide // 2
    me_w, me_n = lax.axis_index("wide"), lax.axis_index("narrow")
    where = jnp.stack([me_w, me_n]).astype(jnp.int32)
    blocks, per_block = block_tiles.shape[0], block_tiles.shape[2]
    slots = blocks // 2 * per_block
    share = slots // narrow // GROUPS
    width = features // HALVES

    far = [swap(hidden, "wide", 2 * chip) for chip in range(chips)]

    local_ids = targets - me_w * vocab_here
    inside = (local_ids >= 0) & (local_ids < vocab_here)
    clipped = jnp.clip(local_ids, 0, vocab_here - 1)
    target_rows = head_weight.at[clipped].get(mode="promise_in_bounds")

    def over_lanes(x):
        return jnp.broadcast_to(x[:, None], (blocks * TILE, TILE))

    far[1], target_rows = lax.optimization_barrier((far[1], target_rows))
    near = [swap(part, "wide", 1) for part in far]
    lse_rows, weight_rows = over_lanes(lse), over_lanes(loss_weight)
    factor = over_lanes(jnp.where(inside, loss_weight, 0.0))
    counts, target_rows, lse_rows, weight_rows, factor = lax.optimization_barrier(
        (block_counts, target_rows, lse_rows, weight_rows, factor)
    )
    slot_blocks, slot_tiles, live = call(
        functools.partial(slots_kernel, slots),
        [shape_of((slots,), jnp.int32)] * 2 + [shape_of((1,), jnp.int32)],
        [SMEM, SMEM],
        (block_tiles, counts),
        0,
        slots * 8,
        scalars=3,
    )
    parts = [part for pair in zip(far, near) for part in pair]

    units = gate_pre.shape[1]
    last_keys = [(k, HALVES - 1) for k in range(2, narrow)]
    probs, tiles = [], []
    for group in range(GROUPS):
        *result, tile = call(
            functools.partial(logits_kernel, wide, narrow, slots, group),
            [shape_of((share * TILE, TILE), f32)]
            + [shape_of((share * TILE + PAD, TILE), i16)] * (narrow - 1)
            + [shape_of((slots // GROUPS * TILE, features), bf16)],
            [SMEM] * 3 + [HBM] + [ANY] * wide,
            (slot_blocks, slot_tiles, where, head_weight, *parts),
            2 * slots * TILE * TILE * features // GROUPS,
            slots * TILE * features,
            [
                pltpu.VMEM((wide, TILE, features), bf16),
                pltpu.SemaphoreType.DMA((wide,)),
                pltpu.SemaphoreType.DMA((slots // GROUPS,)),
            ],
            MEDIUM,
        )
        tiles.append(tile)
        own, *sends = result
        recvs = [swap(send, "narrow", k + 1) for k, send in enumerate(sends)]
        (prob,) = call(
            functools.partial(probs_kernel, narrow, slots, group),
            [shape_of((share * TILE, TILE), bf16)],
            [SMEM] * 3 + [VMEM] * (narrow + 2),
            (slot_blocks, live, where, own, *recvs, lse_rows, weight_rows),
            share * TILE * TILE * 20,
            share * TILE * TILE * 12,
        )
        probs.append([swap(prob, "narrow", k) for k in range(narrow)])
    (held,) = call(
        functools.partial(hold_kernel, last_keys),
        [shape_of((len(last_keys), units, width), bf16)],
        [SMEM, HBM],
        (where, down_weight),
        0,
        len(last_keys) * units * width * 2,
        [pltpu.SemaphoreType.DMA((len(last_keys),))],
        MEDIUM,
    )
    tiles[0], held = lax.optimization_barrier((tiles[0], held))
    all_probs = [probs[group][k] for k in range(narrow) for group in range(GROUPS)]

    halves = []
    for half in range(HALVES):
        mine, other = call(
            functools.partial(grads_kernel, wide, narrow, slots, half),
            [shape_of((chips * TILE, width), f32)] * 2,
            [SMEM] * 2 + [VMEM] * (narrow * GROUPS + GROUPS + 2),
            (slot_blocks, where, *all_probs, *tiles, target_rows, factor),
            2 * slots * TILE * TILE * width,
            slots * TILE * width * 4,
            [pltpu.VMEM((wide, TILE, width), f32)],
        )
        halves.append((mine, swap(other, "wide", 1)))
    grads = []
    for half, (mine, other) in enumerate(halves):
        if half > 0:
            mine, grads[-1] = lax.optimization_barrier((mine, grads[-1]))
        kept, *packed = call(
            functools.partial(pack_kernel, chips),
            [shape_of((TILE, width), f32)]
            + [shape_of((TILE + PAD, width), i16)] * (chips - 1),
            [VMEM] * 2,
            (mine, other),
            chips * TILE * width * 8,
            chips * TILE * width * 10,
        )
        arrived = [swap(part, "wide", 2 * (k + 1)) for k, part in enumerate(packed)]
        (grad,) = call(
            merge_kernel,
            [shape_of((TILE, width), bf16)],
            [VMEM] * chips,
            (kept, *arrived),
            chips * TILE * width * 4,
            chips * TILE * width * 3,
        )
        grads.append(grad)

    pieces = {
        (k, half): (swap(grad, "narrow", k),)
        for half, grad in enumerate(grads)
        for k in range(narrow)
    }
    if narrow == 4:
        near_ends = lax.ppermute(grads[0], "narrow", [(1, 2), (2, 1)])
        ends = lax.ppermute(pieces[2, 0][0], "narrow", [(1, 0), (2, 3)])
        pieces[3, 0] = (near_ends, ends)
    chunk = units // 2 if units // 2 % TILE == 0 else units

    def unit(keys, kind, *extra):
        count = len(keys)
        last = kind == "last"
        inputs = [part for key in keys for part in pieces[key]]
        outs = [shape_of((TILE, units), f32)]
        if kind == "first":
            outs.append(shape_of((TILE, features), bf16))
        if last:
            outs = [shape_of((TILE, units), bf16)] * 2
        return call(
            functools.partial(unit_kernel, keys, [len(pieces[key]) for key in keys], kind, chunk),
            outs,
            [SMEM] + [VMEM] * len(inputs) + [VMEM if last else HBM] + [VMEM] * len(extra),
            (where, *inputs, held if last else down_weight, *extra),
            2 * count * TILE * units * width,
            count * units * width * 2,
            ()
            if last
            else (
                pltpu.VMEM((units // chunk, count, chunk, width), bf16),
                pltpu.SemaphoreType.DMA((units // chunk, count)),
            ),
            16 if last else LARGE,
        )

    summed, head_grad = unit([(0, half) for half in range(HALVES)], "first")
    (summed,) = unit([(k, 0) for k in range(1, narrow)], "more", summed)
    (summed,) = unit([(1, 1)], "more", summed)
    gate_grad, up_grad = unit(last_keys, "last", summed, gate_pre, up_pre)
    return head_grad, gate_grad, up_grad


def solution(mesh):
    in_specs = (
        P("wide", "narrow"),
        P("wide", "narrow"),
        P(),
        P(),
        P(),
        P(None, "wide", None),
        P(None, "wide"),
        P("wide", "narrow"),
        P("wide", "narrow"),
        P("narrow", None),
    )
    out_specs = (P("wide", "narrow"), P("wide", "narrow"), P("wide", "narrow"))

    return jax.shard_map(
        on_device, mesh=mesh, in_specs=in_specs, out_specs=out_specs, check_vma=False
    )
```

```python
import functools

import jax
import jax.numpy as jnp
from jax import lax
from jax.experimental import pallas as pl
from jax.experimental.pallas import tpu as pltpu
from jax.sharding import PartitionSpec as P


TILE = 128
PAD = 8
GROUPS = 2
HALVES = 2
LARGE = 50
MEDIUM = 46
LEVELS = 32767.0
VMEM = pl.BlockSpec(memory_space=pltpu.VMEM)
SMEM = pl.BlockSpec(memory_space=pltpu.SMEM)
ANY = pl.BlockSpec(memory_space=pl.ANY)
HBM = pl.BlockSpec(memory_space=pltpu.HBM)


def swap(x, axis, mask):
    if mask == 0:
        return x
    size = lax.axis_size(axis)
    return lax.ppermute(x, axis, [(i, i ^ mask) for i in range(size)])


def step_of(code):
    return jnp.exp2(code * 0.125) * (1.0 / LEVELS)


def encode(x):
    peak = jnp.max(jnp.abs(x), axis=0, keepdims=True)
    code = jnp.ceil(8.0 * jnp.log2(jnp.maximum(peak, 1e-30)) + 0.25)
    levels = jnp.round(x * (1.0 / step_of(code)))
    return levels.astype(jnp.int32).astype(jnp.int16), code.astype(jnp.int32)


def decode(levels, code):
    return levels.astype(jnp.int32).astype(jnp.float32) * step_of(code.astype(jnp.float32))


def tiles_kernel(slots, tiles_ref, counts_ref, head, blocks_out, tiles_out, live_out, out, sem):
    blocks, _, per_block = tiles_ref.shape

    def copy(tile, slot):
        return pltpu.make_async_copy(
            head.at[pl.ds(pl.multiple_of(tile * TILE, TILE), TILE), :],
            out.at[pl.ds(pl.multiple_of(slot * TILE, TILE), TILE), :],
            sem.at[slot],
        )

    def place(slot, block, tile):
        blocks_out[slot] = block
        tiles_out[slot] = tile
        copy(tile, slot).start()

    live = jnp.int32(0)
    for block in range(blocks):
        count = counts_ref[block, 0]
        for j in range(per_block):
            pl.when(j < count)(
                functools.partial(place, live + j, block, tiles_ref[block, 0, j])
            )
        live = live + count
    live_out[0] = live
    for slot in range(slots):
        pl.when(slot >= live)(functools.partial(place, slot, 0, 0))
    for slot in range(slots):
        copy(0, slot).wait()


def logits_kernel(wide, narrow, slots, group, blocks_ref, where_ref, tiles, *refs):
    me_w, me_n = where_ref[0], where_ref[1]
    per = slots // narrow
    share = per // GROUPS
    parts, own, sends = refs[:wide], refs[wide], refs[wide + 1 : wide + narrow]
    rows, sem = refs[wide + narrow :]
    copies = [pltpu.make_async_copy(parts[k], rows.at[k], sem.at[k]) for k in range(wide)]
    for copy in copies:
        copy.start()
    for send in sends:
        send[share * TILE :, :] = jnp.zeros((send.shape[0] - share * TILE, TILE), jnp.int16)
    for copy in copies:
        copy.wait()
    for k in [*range(1, narrow), 0]:
        for i in range(share):
            slot = (me_n ^ k) * per + group * share + i
            part = lax.dot_general(
                rows[blocks_ref[slot] ^ me_w],
                tiles[pl.ds(pl.multiple_of(slot * TILE, TILE), TILE), :],
                (((1,), (1,)), ((), ())),
                preferred_element_type=jnp.float32,
            )
            if k == 0:
                own[i * TILE : (i + 1) * TILE, :] = part
            else:
                levels, code = encode(part)
                sends[k - 1][i * TILE : (i + 1) * TILE, :] = levels
                sends[k - 1][share * TILE + i : share * TILE + i + 1, :] = code.astype(jnp.int16)


def probs_kernel(narrow, slots, group, blocks_ref, live_ref, where_ref, own, *refs):
    recvs, lse, weight, out = refs[: narrow - 1], refs[-3], refs[-2], refs[-1]
    per = slots // narrow
    share = per // GROUPS
    codes = [recv[share * TILE :, :] for recv in recvs]
    for i in range(share):
        slot = where_ref[1] * per + group * share + i
        total = own[i * TILE : (i + 1) * TILE, :]
        for recv, code in zip(recvs, codes):
            total = total + decode(recv[i * TILE : (i + 1) * TILE, :], code[i : i + 1, :])
        rows = pl.ds(pl.multiple_of(blocks_ref[slot] * TILE, TILE), TILE)
        scaled = jnp.exp(total - lse[rows, :]) * weight[rows, :]
        out[i * TILE : (i + 1) * TILE, :] = jnp.where(slot < live_ref[0], scaled, 0.0).astype(
            jnp.bfloat16
        )


def grads_kernel(wide, narrow, slots, half, blocks_ref, tiles_ref, where_ref, head, *refs):
    probs = refs[: narrow * GROUPS]
    target_rows, factor, mine, other, total, tiles, sem = refs[narrow * GROUPS :]
    me_w, me_n = where_ref[0], where_ref[1]
    per = slots // narrow
    share = per // GROUPS
    width = mine.shape[1]

    def fetch(slot):
        start = pl.multiple_of(tiles_ref[slot] * TILE, TILE)
        part = head.at[pl.ds(start, TILE), pl.ds(half * width, width)]
        return pltpu.make_async_copy(part, tiles.at[slot], sem.at[slot])

    for slot in range(slots):
        fetch(slot).start()
    for block in range(factor.shape[0] // TILE):
        rows = slice(block * TILE, (block + 1) * TILE)
        weight = -factor[rows, :]
        for lane in range(0, width, TILE):
            at = half * width + lane
            total[block ^ me_w, :, lane : lane + TILE] = weight * target_rows[
                rows, at : at + TILE
            ].astype(jnp.float32)
    for slot in range(slots):
        fetch(slot).wait()
    for k in range(narrow):
        for group in range(GROUPS):
            for i in range(share):
                slot = (me_n ^ k) * per + group * share + i
                total[blocks_ref[slot] ^ me_w] += jnp.dot(
                    probs[k * GROUPS + group][i * TILE : (i + 1) * TILE, :],
                    tiles[slot],
                    preferred_element_type=jnp.float32,
                )
    for chip in range(wide // 2):
        mine[chip * TILE : (chip + 1) * TILE, :] = total[2 * chip]
        other[chip * TILE : (chip + 1) * TILE, :] = total[2 * chip + 1]


def pack_kernel(chips, mine, other, own, *sends):
    for chip in [*range(1, chips), 0]:
        rows = slice(chip * TILE, (chip + 1) * TILE)
        if chip == 0:
            own[...] = mine[rows, :] + other[rows, :]
            continue
        send = sends[chip - 1]
        for lane in range(0, own.shape[1], TILE):
            lanes = slice(lane, lane + TILE)
            levels, code = encode(mine[rows, lanes] + other[rows, lanes])
            send[:TILE, lanes] = levels
            send[TILE:, lanes] = jnp.broadcast_to(code, (PAD, TILE)).astype(jnp.int16)


def merge_kernel(chips, before, own, *refs):
    recvs, befores, outs = refs[: chips - 1], refs[chips - 1 : chips - 1 + before], refs[-1 - before :]
    width = own.shape[1]
    for lane in range(0, width, TILE):
        lanes = slice(lane, lane + TILE)
        total = own[:, lanes]
        for recv in recvs:
            total = total + decode(recv[:TILE, lanes], recv[TILE : TILE + 1, lanes])
        outs[0][:, lanes] = total.astype(jnp.bfloat16)
    if before:
        for at, part in enumerate([*befores, outs[0]]):
            outs[1][:, at * width : (at + 1) * width] = part[...]


def down_copies(keys, where_ref, down, out, sem, rows):
    width = out.shape[-1]

    def copy(at):
        mask, half = keys[at]
        start = pl.multiple_of((where_ref[1] ^ mask) * (width * HALVES) + half * width, width)
        return pltpu.make_async_copy(down.at[rows, pl.ds(start, width)], out.at[at], sem.at[at])

    return [copy(at) for at in range(len(keys))]


def hold_kernel(keys, where_ref, down, out, sem):
    copies = down_copies(keys, where_ref, down, out, sem, slice(None))
    for copy in copies:
        copy.start()
    for copy in copies:
        copy.wait()


def unit_kernel(keys, splits, kind, chunk, skip, where_ref, *refs):
    count, inputs = len(keys), sum(splits)
    arrived, down, refs = list(refs[:inputs]), refs[inputs], list(refs[inputs + 1 :])
    units = down.shape[-2]
    pieces = []
    for split in splits:
        piece = arrived.pop(0)[...]
        for _ in range(split - 1):
            piece = piece + arrived.pop(0)[...]
        pieces.append(piece)
    summed = None if kind == "first" else refs.pop(0)
    if kind == "last":
        gate, up, gate_out, up_out = refs[:4]
    else:
        sum_out = refs[0]
    steps = [pl.ds(at, chunk) for at in range(0, units, chunk)]
    if skip is None:
        down_v, sem = refs[-2:]
        copies = [
            down_copies(keys, where_ref, down, down_v.at[step], sem.at[step], rows)
            for step, rows in enumerate(steps)
        ]
        for copy in sum(copies, []):
            copy.start()
    for step, rows in enumerate(steps):
        total = None if summed is None else summed[:, rows]
        for at in range(count):
            if skip is None:
                copies[step][at].wait()
            part = lax.dot_general(
                pieces[at],
                down_v[step, at] if skip is None else down[skip + at, rows, :],
                (((1,), (1,)), ((), ())),
                preferred_element_type=jnp.float32,
            )
            total = part if total is None else total + part
        if kind != "last":
            sum_out[:, rows] = total
            continue
        g = gate[:, rows].astype(jnp.float32)
        u = up[:, rows].astype(jnp.float32)
        s = 1.0 / (1.0 + jnp.exp(-g))
        up_out[:, rows] = (total * g * s).astype(jnp.bfloat16)
        gate_out[:, rows] = (total * u * s * (1.0 + g * (1.0 - s))).astype(jnp.bfloat16)


def shape_of(shape, dtype):
    return jax.ShapeDtypeStruct(shape, dtype)


def call(kernel, outs, ins, args, flops, moved, scratch=(), mib=16, scalars=0):
    return pl.pallas_call(
        kernel,
        out_shape=outs,
        in_specs=ins,
        out_specs=[SMEM] * scalars + [VMEM] * (len(outs) - scalars),
        scratch_shapes=list(scratch),
        compiler_params=pltpu.CompilerParams(vmem_limit_bytes=mib * 1024 * 1024),
        cost_estimate=pl.CostEstimate(flops=flops, bytes_accessed=moved, transcendentals=0),
    )(*args)


def on_device(
    hidden,
    head_weight,
    lse,
    targets,
    loss_weight,
    block_tiles,
    block_counts,
    gate_pre,
    up_pre,
    down_weight,
):
    f32, bf16, i16 = jnp.float32, jnp.bfloat16, jnp.int16
    _, features = hidden.shape
    vocab_here = head_weight.shape[0]
    wide, narrow = lax.axis_size("wide"), lax.axis_size("narrow")
    chips = wide // 2
    me_w, me_n = lax.axis_index("wide"), lax.axis_index("narrow")
    where = jnp.stack([me_w, me_n]).astype(jnp.int32)
    blocks, per_block = block_tiles.shape[0], block_tiles.shape[2]
    slots = blocks // 2 * per_block
    share = slots // narrow // GROUPS
    width = features // HALVES

    far = [swap(hidden, "wide", 2 * chip) for chip in range(chips)]

    local_ids = targets - me_w * vocab_here
    inside = (local_ids >= 0) & (local_ids < vocab_here)
    clipped = jnp.clip(local_ids, 0, vocab_here - 1)

    def over_lanes(x):
        return jnp.broadcast_to(x[:, None], (blocks * TILE, TILE))

    lse_rows, weight_rows = over_lanes(lse), over_lanes(loss_weight)
    factor = over_lanes(jnp.where(inside, loss_weight, 0.0))
    counts, where, lse_rows, weight_rows, factor = lax.optimization_barrier(
        (block_counts, where, lse_rows, weight_rows, factor)
    )
    slot_blocks, slot_tiles, live, tiles = call(
        functools.partial(tiles_kernel, slots),
        [shape_of((slots,), jnp.int32)] * 2
        + [shape_of((1,), jnp.int32), shape_of((slots * TILE, features), bf16)],
        [SMEM, SMEM, HBM],
        (block_tiles, counts, head_weight),
        0,
        slots * TILE * features * 2,
        [pltpu.SemaphoreType.DMA((slots,))],
        MEDIUM,
        3,
    )
    far[1], tiles = lax.optimization_barrier((far[1], tiles))
    near = [swap(part, "wide", 1) for part in far]
    parts = [part for pair in zip(far, near) for part in pair]

    probs = []
    for group in range(GROUPS):
        result = call(
            functools.partial(logits_kernel, wide, narrow, slots, group),
            [shape_of((share * TILE, TILE), f32)]
            + [shape_of((share * TILE + PAD, TILE), i16)] * (narrow - 1),
            [SMEM] * 2 + [VMEM] + [ANY] * wide,
            (slot_blocks, where, tiles, *parts),
            2 * slots * TILE * TILE * features // GROUPS,
            slots * TILE * features,
            [pltpu.VMEM((wide, TILE, features), bf16), pltpu.SemaphoreType.DMA((wide,))],
        )
        own, *sends = result
        recvs = [swap(send, "narrow", k + 1) for k, send in enumerate(sends)]
        (prob,) = call(
            functools.partial(probs_kernel, narrow, slots, group),
            [shape_of((share * TILE, TILE), bf16)],
            [SMEM] * 3 + [VMEM] * (narrow + 2),
            (slot_blocks, live, where, own, *recvs, lse_rows, weight_rows),
            share * TILE * TILE * 20,
            share * TILE * TILE * 12,
        )
        if group == GROUPS - 1:
            prob, clipped = lax.optimization_barrier((prob, clipped))
        probs.append([swap(prob, "narrow", k) for k in range(narrow)])
    target_rows = head_weight.at[clipped].get(mode="promise_in_bounds")
    all_probs = [probs[group][k] for k in range(narrow) for group in range(GROUPS)]

    halves = []
    for half in range(HALVES):
        mine, other = call(
            functools.partial(grads_kernel, wide, narrow, slots, half),
            [shape_of((chips * TILE, width), f32)] * 2,
            [SMEM] * 3 + [HBM] + [VMEM] * (narrow * GROUPS + 2),
            (slot_blocks, slot_tiles, where, head_weight, *all_probs, target_rows, factor),
            2 * slots * TILE * TILE * width,
            slots * TILE * width * 4,
            [
                pltpu.VMEM((wide, TILE, width), f32),
                pltpu.VMEM((slots, TILE, width), bf16),
                pltpu.SemaphoreType.DMA((slots,)),
            ],
            MEDIUM,
        )
        halves.append((mine, swap(other, "wide", 1)))
    units = gate_pre.shape[1]
    held_keys = [(k, HALVES - 1) for k in range(1, narrow)]
    chunk = units // 2 if units // 2 % TILE == 0 else units

    def unit(keys, kind, skip, *extra):
        last = kind == "last"
        inputs = [part for key in keys for part in pieces[key]]
        count = len(keys)
        return call(
            functools.partial(
                unit_kernel, keys, [len(pieces[key]) for key in keys], kind, chunk, skip
            ),
            [shape_of((TILE, units), bf16)] * 2 if last else [shape_of((TILE, units), f32)],
            [SMEM]
            + [VMEM] * len(inputs)
            + [HBM if skip is None else VMEM]
            + [VMEM] * len(extra),
            (where, *inputs, down_weight if skip is None else held, *extra),
            2 * count * TILE * units * width,
            count * units * width * 2,
            (
                pltpu.VMEM((units // chunk, count, chunk, width), bf16),
                pltpu.SemaphoreType.DMA((units // chunk, count)),
            )
            if skip is None
            else (),
            LARGE if skip is None else 16,
        )

    pieces = {}
    grads = []
    for half, (mine, other) in enumerate(halves):
        if half > 0:
            mine, grads[-1] = lax.optimization_barrier((mine, grads[-1]))
        kept, *packed = call(
            functools.partial(pack_kernel, chips),
            [shape_of((TILE, width), f32)]
            + [shape_of((TILE + PAD, width), i16)] * (chips - 1),
            [VMEM] * 2,
            (mine, other),
            chips * TILE * width * 8,
            chips * TILE * width * 10,
        )
        arrived = [swap(part, "wide", 2 * (k + 1)) for k, part in enumerate(packed)]
        if half == 0:
            kept, here = lax.optimization_barrier((kept, where))
            (held,) = call(
                functools.partial(hold_kernel, held_keys),
                [shape_of((len(held_keys), units, width), bf16)],
                [SMEM, HBM],
                (here, down_weight),
                0,
                len(held_keys) * units * width * 2,
                [pltpu.SemaphoreType.DMA((len(held_keys),))],
                MEDIUM,
            )
            kept, held = lax.optimization_barrier((kept, held))
        if half == HALVES - 1:
            (summed,) = unit([(0, at) for at in range(half)], "first", None)
            kept, summed = lax.optimization_barrier((kept, summed))
        before = list(grads) if half == HALVES - 1 else []
        full = [shape_of((TILE, features), bf16)] if before else []
        grad, *head_grad = call(
            functools.partial(merge_kernel, chips, len(before)),
            [shape_of((TILE, width), bf16)] + full,
            [VMEM] * (chips + len(before)),
            (kept, *arrived, *before),
            chips * TILE * width * 4,
            chips * TILE * width * 3,
        )
        grads.append(grad)
        for k in range(narrow):
            pieces[k, half] = (swap(grad, "narrow", k),)

    if narrow == 4:
        near_ends = lax.ppermute(grads[0], "narrow", [(1, 2), (2, 1)])
        ends = lax.ppermute(pieces[2, 0][0], "narrow", [(1, 0), (2, 3)])
        pieces[3, 0] = (near_ends, ends)
    (summed,) = unit([(0, 1), *[(k, 0) for k in range(1, narrow)]], "more", None, summed)
    (summed,) = unit(held_keys[:1], "more", 0, summed)
    gate_grad, up_grad = unit(held_keys[1:], "last", 1, summed, gate_pre, up_pre)
    (head_grad,) = head_grad
    return head_grad, gate_grad, up_grad


def solution(mesh):
    in_specs = (
        P("wide", "narrow"),
        P("wide", "narrow"),
        P(),
        P(),
        P(),
        P(None, "wide", None),
        P(None, "wide"),
        P("wide", "narrow"),
        P("wide", "narrow"),
        P("narrow", None),
    )
    out_specs = (P("wide", "narrow"), P("wide", "narrow"), P("wide", "narrow"))

    return jax.shard_map(
        on_device, mesh=mesh, in_specs=in_specs, out_specs=out_specs, check_vma=False
    )
```

```python
import functools

import jax
import jax.numpy as jnp
from jax import lax
from jax.experimental import pallas as pl
from jax.experimental.pallas import tpu as pltpu
from jax.sharding import PartitionSpec as P


TILE = 128
PAD = 8
GROUPS = 2
HALVES = 2
GROUP_ROWS = 8
AT_ONCE = 32
LARGE = 50
MEDIUM = 46
LEVELS = 32767.0
VMEM = pl.BlockSpec(memory_space=pltpu.VMEM)
SMEM = pl.BlockSpec(memory_space=pltpu.SMEM)
ANY = pl.BlockSpec(memory_space=pl.ANY)
HBM = pl.BlockSpec(memory_space=pltpu.HBM)


def swap(x, axis, mask):
    if mask == 0:
        return x
    size = lax.axis_size(axis)
    return lax.ppermute(x, axis, [(i, i ^ mask) for i in range(size)])


def step_of(code):
    return jnp.exp2(code * 0.125) * (1.0 / LEVELS)


def encode(x):
    peak = jnp.max(jnp.abs(x), axis=0, keepdims=True)
    code = jnp.ceil(8.0 * jnp.log2(jnp.maximum(peak, 1e-30)) + 0.25)
    levels = jnp.round(x * (1.0 / step_of(code)))
    return levels.astype(jnp.int32).astype(jnp.int16), code.astype(jnp.int32)


def decode(levels, code):
    return levels.astype(jnp.int32).astype(jnp.float32) * step_of(code.astype(jnp.float32))


def tiles_kernel(slots, tiles_ref, counts_ref, head, blocks_out, live_out, out, sem):
    blocks, _, per_block = tiles_ref.shape

    def copy(tile, slot):
        return pltpu.make_async_copy(
            head.at[pl.ds(pl.multiple_of(tile * TILE, TILE), TILE), :],
            out.at[pl.ds(pl.multiple_of(slot * TILE, TILE), TILE), :],
            sem.at[slot],
        )

    def place(slot, block, tile):
        blocks_out[slot] = block
        copy(tile, slot).start()

    live = jnp.int32(0)
    for block in range(blocks):
        count = counts_ref[block, 0]
        for j in range(per_block):
            pl.when(j < count)(
                functools.partial(place, live + j, block, tiles_ref[block, 0, j])
            )
        live = live + count
    live_out[0] = live
    for slot in range(slots):
        pl.when(slot >= live)(functools.partial(place, slot, 0, 0))
    for slot in range(slots):
        copy(0, slot).wait()


def logits_kernel(wide, narrow, slots, group, blocks_ref, where_ref, tiles, *refs):
    me_w, me_n = where_ref[0], where_ref[1]
    per = slots // narrow
    share = per // GROUPS
    parts, own, sends = refs[:wide], refs[wide], refs[wide + 1 : wide + narrow]
    rows, sem = refs[wide + narrow :]
    copies = [pltpu.make_async_copy(parts[k], rows.at[k], sem.at[k]) for k in range(wide)]
    for copy in copies:
        copy.start()
    for send in sends:
        send[share * TILE :, :] = jnp.zeros((send.shape[0] - share * TILE, TILE), jnp.int16)
    for copy in copies:
        copy.wait()
    for k in [*range(1, narrow), 0]:
        for i in range(share):
            slot = (me_n ^ k) * per + group * share + i
            part = lax.dot_general(
                rows[blocks_ref[slot] ^ me_w],
                tiles[pl.ds(pl.multiple_of(slot * TILE, TILE), TILE), :],
                (((1,), (1,)), ((), ())),
                preferred_element_type=jnp.float32,
            )
            if k == 0:
                own[i * TILE : (i + 1) * TILE, :] = part
            else:
                levels, code = encode(part)
                sends[k - 1][i * TILE : (i + 1) * TILE, :] = levels
                sends[k - 1][share * TILE + i : share * TILE + i + 1, :] = code.astype(jnp.int16)


def targets_kernel(list_ref, count_ref, code, head, out, groups, more, sem, more_sem):
    blocks = code.shape[0]

    def copy(block, j, buffer, at, sem):
        start = pl.multiple_of(list_ref[block * TILE + j] * GROUP_ROWS, GROUP_ROWS)
        return pltpu.make_async_copy(
            head.at[pl.ds(start, GROUP_ROWS), :],
            buffer.at[pl.ds(pl.multiple_of(at * GROUP_ROWS, GROUP_ROWS), GROUP_ROWS), :],
            sem,
        )

    def place(block, chunk, buffer):
        depth = AT_ONCE * GROUP_ROWS
        wanted = code[block : block + 1, :] - chunk * depth
        spot = lax.broadcasted_iota(jnp.int32, (depth, TILE), 0)
        hit = jnp.where(spot == wanted, 1.0, 0.0).astype(jnp.bfloat16)
        return lax.dot_general(
            hit, buffer[...], (((0,), (0,)), ((), ())), preferred_element_type=jnp.float32
        )

    for block in range(blocks):
        for j in range(AT_ONCE):
            copy(block, j, groups.at[block], j, sem.at[block]).start()
    for block in range(blocks):
        rows = pl.ds(block * TILE, TILE)
        pltpu.make_async_copy(
            head.at[pl.ds(0, AT_ONCE * GROUP_ROWS), :], groups.at[block], sem.at[block]
        ).wait()
        out[rows, :] = place(block, 0, groups.at[block]).astype(jnp.bfloat16)

        @pl.when(count_ref[block] > AT_ONCE)
        def _(block=block, rows=rows):
            def body(chunk, carry):
                def start(j, carry):
                    copy(block, chunk * AT_ONCE + j, more, j, more_sem).start()
                    return carry

                lax.fori_loop(0, AT_ONCE, start, 0)
                pltpu.make_async_copy(
                    head.at[pl.ds(0, AT_ONCE * GROUP_ROWS), :], more, more_sem
                ).wait()
                added = out[rows, :].astype(jnp.float32) + place(block, chunk, more)
                out[rows, :] = added.astype(jnp.bfloat16)
                return carry

            lax.fori_loop(1, (count_ref[block] + AT_ONCE - 1) // AT_ONCE, body, 0)


def probs_kernel(narrow, slots, group, blocks_ref, live_ref, where_ref, own, *refs):
    recvs, lse, weight, out = refs[: narrow - 1], refs[-3], refs[-2], refs[-1]
    per = slots // narrow
    share = per // GROUPS
    codes = [recv[share * TILE :, :] for recv in recvs]
    for i in range(share):
        slot = where_ref[1] * per + group * share + i
        total = own[i * TILE : (i + 1) * TILE, :]
        for recv, code in zip(recvs, codes):
            total = total + decode(recv[i * TILE : (i + 1) * TILE, :], code[i : i + 1, :])
        rows = pl.ds(pl.multiple_of(blocks_ref[slot] * TILE, TILE), TILE)
        scaled = jnp.exp(total - lse[rows, :]) * weight[rows, :]
        out[i * TILE : (i + 1) * TILE, :] = jnp.where(slot < live_ref[0], scaled, 0.0).astype(
            jnp.bfloat16
        )


def grads_kernel(wide, narrow, slots, half, blocks_ref, where_ref, tiles, *refs):
    probs = refs[: narrow * GROUPS]
    target_rows, factor, mine, other, total = refs[narrow * GROUPS :]
    me_w, me_n = where_ref[0], where_ref[1]
    per = slots // narrow
    share = per // GROUPS
    width = mine.shape[1]
    for block in range(factor.shape[0] // TILE):
        rows = slice(block * TILE, (block + 1) * TILE)
        weight = -factor[rows, :]
        for lane in range(0, width, TILE):
            at = half * width + lane
            total[block ^ me_w, :, lane : lane + TILE] = weight * target_rows[
                rows, at : at + TILE
            ].astype(jnp.float32)
    for k in range(narrow):
        for group in range(GROUPS):
            for i in range(share):
                slot = (me_n ^ k) * per + group * share + i
                total[blocks_ref[slot] ^ me_w] += jnp.dot(
                    probs[k * GROUPS + group][i * TILE : (i + 1) * TILE, :],
                    tiles[
                        pl.ds(pl.multiple_of(slot * TILE, TILE), TILE),
                        half * width : (half + 1) * width,
                    ],
                    preferred_element_type=jnp.float32,
                )
    for chip in range(wide // 2):
        mine[chip * TILE : (chip + 1) * TILE, :] = total[2 * chip]
        other[chip * TILE : (chip + 1) * TILE, :] = total[2 * chip + 1]


def pack_kernel(chips, mine, other, own, *sends):
    for chip in [*range(1, chips), 0]:
        rows = slice(chip * TILE, (chip + 1) * TILE)
        if chip == 0:
            own[...] = mine[rows, :] + other[rows, :]
            continue
        send = sends[chip - 1]
        for lane in range(0, own.shape[1], TILE):
            lanes = slice(lane, lane + TILE)
            levels, code = encode(mine[rows, lanes] + other[rows, lanes])
            send[:TILE, lanes] = levels
            send[TILE:, lanes] = jnp.broadcast_to(code, (PAD, TILE)).astype(jnp.int16)


def merge_kernel(own, *refs):
    recvs, out = refs[:-1], refs[-1]
    for lane in range(0, own.shape[1], TILE):
        lanes = slice(lane, lane + TILE)
        total = own[:, lanes]
        for recv in recvs:
            total = total + decode(recv[:TILE, lanes], recv[TILE : TILE + 1, lanes])
        out[:, lanes] = total.astype(jnp.bfloat16)


def down_copies(keys, where_ref, down, out, sem, rows):
    width = out.shape[-1]

    def copy(at):
        mask, half = keys[at]
        start = pl.multiple_of((where_ref[1] ^ mask) * (width * HALVES) + half * width, width)
        return pltpu.make_async_copy(down.at[rows, pl.ds(start, width)], out.at[at], sem.at[at])

    return [copy(at) for at in range(len(keys))]


def hold_kernel(keys, where_ref, down, out, sem):
    copies = down_copies(keys, where_ref, down, out, sem, slice(None))
    for copy in copies:
        copy.start()
    for copy in copies:
        copy.wait()


def unit_kernel(keys, splits, kind, chunk, skip, where_ref, *refs):
    count, inputs = len(keys), sum(splits)
    arrived, down, refs = list(refs[:inputs]), refs[inputs], list(refs[inputs + 1 :])
    units = down.shape[-2]
    width = arrived[0].shape[1]
    pieces = []
    for split in splits:
        piece = arrived.pop(0)[...]
        for _ in range(split - 1):
            piece = piece + arrived.pop(0)[...]
        pieces.append(piece)
    summed = None if kind == "first" else refs.pop(0)
    if kind == "last":
        gate, up, gate_out, up_out = refs[:4]
    else:
        sum_out = refs[0]
    if kind == "first":
        for at in range(HALVES):
            refs[1][:, at * width : (at + 1) * width] = pieces[at]
    steps = [pl.ds(at, chunk) for at in range(0, units, chunk)]
    if skip is None:
        down_v, sem = refs[-2:]
        copies = [
            down_copies(keys, where_ref, down, down_v.at[step], sem.at[step], rows)
            for step, rows in enumerate(steps)
        ]
        for copy in sum(copies, []):
            copy.start()
    for step, rows in enumerate(steps):
        total = None if summed is None else summed[:, rows]
        for at in range(count):
            if skip is None:
                copies[step][at].wait()
            part = lax.dot_general(
                pieces[at],
                down_v[step, at] if skip is None else down[skip + at, rows, :],
                (((1,), (1,)), ((), ())),
                preferred_element_type=jnp.float32,
            )
            total = part if total is None else total + part
        if kind != "last":
            sum_out[:, rows] = total
            continue
        g = gate[:, rows].astype(jnp.float32)
        u = up[:, rows].astype(jnp.float32)
        s = 1.0 / (1.0 + jnp.exp(-g))
        up_out[:, rows] = (total * g * s).astype(jnp.bfloat16)
        gate_out[:, rows] = (total * u * s * (1.0 + g * (1.0 - s))).astype(jnp.bfloat16)


def shape_of(shape, dtype):
    return jax.ShapeDtypeStruct(shape, dtype)


def call(kernel, outs, ins, args, flops, moved, scratch=(), mib=16, scalars=0):
    return pl.pallas_call(
        kernel,
        out_shape=outs,
        in_specs=ins,
        out_specs=[SMEM] * scalars + [VMEM] * (len(outs) - scalars),
        scratch_shapes=list(scratch),
        compiler_params=pltpu.CompilerParams(vmem_limit_bytes=mib * 1024 * 1024),
        cost_estimate=pl.CostEstimate(flops=flops, bytes_accessed=moved, transcendentals=0),
    )(*args)


def on_device(
    hidden,
    head_weight,
    lse,
    targets,
    loss_weight,
    block_tiles,
    block_counts,
    gate_pre,
    up_pre,
    down_weight,
):
    f32, bf16, i16 = jnp.float32, jnp.bfloat16, jnp.int16
    _, features = hidden.shape
    vocab_here = head_weight.shape[0]
    wide, narrow = lax.axis_size("wide"), lax.axis_size("narrow")
    chips = wide // 2
    me_w, me_n = lax.axis_index("wide"), lax.axis_index("narrow")
    where = jnp.stack([me_w, me_n]).astype(jnp.int32)
    blocks, per_block = block_tiles.shape[0], block_tiles.shape[2]
    slots = blocks // 2 * per_block
    share = slots // narrow // GROUPS
    width = features // HALVES

    far = [swap(hidden, "wide", 2 * chip) for chip in range(chips)]

    local_ids = (targets - me_w * vocab_here).reshape(blocks, TILE)
    inside = (local_ids >= 0) & (local_ids < vocab_here)
    order = jnp.arange(TILE, dtype=jnp.int32)
    earlier = (order[None, :] < order[:, None])[None] & inside[:, None, :]
    rank = jnp.sum(earlier.astype(jnp.int32), axis=2)
    target_code = jnp.where(inside, rank * GROUP_ROWS + local_ids % GROUP_ROWS, -1)
    chosen = (rank[:, None, :] == order[None, :, None]) & inside[:, None, :]
    target_list = jnp.sum(jnp.where(chosen, (local_ids // GROUP_ROWS)[:, None, :], 0), axis=2)
    target_count = jnp.sum(inside.astype(jnp.int32), axis=1)

    def over_lanes(x):
        return jnp.broadcast_to(x[:, None], (blocks * TILE, TILE))

    lse_rows, weight_rows = over_lanes(lse), over_lanes(loss_weight)
    factor = over_lanes(jnp.where(inside.reshape(-1), loss_weight, 0.0))
    target_list = target_list.reshape(-1)
    counts, where, lse_rows, weight_rows, factor, target_list, target_count, target_code = (
        lax.optimization_barrier(
            (
                *(block_counts, where, lse_rows, weight_rows, factor),
                *(target_list, target_count, target_code),
            )
        )
    )
    slot_blocks, live, tiles = call(
        functools.partial(tiles_kernel, slots),
        [
            shape_of((slots,), jnp.int32),
            shape_of((1,), jnp.int32),
            shape_of((slots * TILE, features), bf16),
        ],
        [SMEM, SMEM, HBM],
        (block_tiles, counts, head_weight),
        0,
        slots * TILE * features * 2,
        [pltpu.SemaphoreType.DMA((slots,))],
        MEDIUM,
        2,
    )
    far[1], tiles = lax.optimization_barrier((far[1], tiles))
    near = [swap(part, "wide", 1) for part in far]
    parts = [part for pair in zip(far, near) for part in pair]

    probs = []
    for group in range(GROUPS):
        result = call(
            functools.partial(logits_kernel, wide, narrow, slots, group),
            [shape_of((share * TILE, TILE), f32)]
            + [shape_of((share * TILE + PAD, TILE), i16)] * (narrow - 1),
            [SMEM] * 2 + [VMEM] + [ANY] * wide,
            (slot_blocks, where, tiles, *parts),
            2 * slots * TILE * TILE * features // GROUPS,
            slots * TILE * features,
            [pltpu.VMEM((wide, TILE, features), bf16), pltpu.SemaphoreType.DMA((wide,))],
        )
        own, *sends = result
        recvs = [swap(send, "narrow", k + 1) for k, send in enumerate(sends)]
        (prob,) = call(
            functools.partial(probs_kernel, narrow, slots, group),
            [shape_of((share * TILE, TILE), bf16)],
            [SMEM] * 3 + [VMEM] * (narrow + 2),
            (slot_blocks, live, where, own, *recvs, lse_rows, weight_rows),
            share * TILE * TILE * 20,
            share * TILE * TILE * 12,
        )
        if group == GROUPS - 1:
            prob, target_code = lax.optimization_barrier((prob, target_code))
        probs.append([swap(prob, "narrow", k) for k in range(narrow)])
    (target_rows,) = call(
        targets_kernel,
        [shape_of((blocks * TILE, features), bf16)],
        [SMEM, SMEM, VMEM, HBM],
        (target_list, target_count, target_code, head_weight),
        2 * blocks * AT_ONCE * GROUP_ROWS * TILE * features,
        blocks * AT_ONCE * GROUP_ROWS * features * 2,
        [
            pltpu.VMEM((blocks, AT_ONCE * GROUP_ROWS, features), bf16),
            pltpu.VMEM((AT_ONCE * GROUP_ROWS, features), bf16),
            pltpu.SemaphoreType.DMA((blocks,)),
            pltpu.SemaphoreType.DMA(()),
        ],
        MEDIUM,
    )
    all_probs = [probs[group][k] for k in range(narrow) for group in range(GROUPS)]

    halves = []
    for half in range(HALVES):
        mine, other = call(
            functools.partial(grads_kernel, wide, narrow, slots, half),
            [shape_of((chips * TILE, width), f32)] * 2,
            [SMEM] * 2 + [VMEM] * (narrow * GROUPS + 3),
            (slot_blocks, where, tiles, *all_probs, target_rows, factor),
            2 * slots * TILE * TILE * width,
            slots * TILE * width * 4,
            [pltpu.VMEM((wide, TILE, width), f32)],
        )
        halves.append((mine, swap(other, "wide", 1)))
    units = gate_pre.shape[1]
    held_keys = [(k, HALVES - 1) for k in range(1, narrow)]
    chunk = units // 2 if units // 2 % TILE == 0 else units

    def unit(keys, kind, skip, *extra):
        last = kind == "last"
        inputs = [part for key in keys for part in pieces[key]]
        count = len(keys)
        return call(
            functools.partial(
                unit_kernel, keys, [len(pieces[key]) for key in keys], kind, chunk, skip
            ),
            [shape_of((TILE, units), bf16)] * 2
            if last
            else [shape_of((TILE, units), f32)]
            + [shape_of((TILE, features), bf16)] * (kind == "first"),
            [SMEM]
            + [VMEM] * len(inputs)
            + [HBM if skip is None else VMEM]
            + [VMEM] * len(extra),
            (where, *inputs, down_weight if skip is None else held, *extra),
            2 * count * TILE * units * width,
            count * units * width * 2,
            (
                pltpu.VMEM((units // chunk, count, chunk, width), bf16),
                pltpu.SemaphoreType.DMA((units // chunk, count)),
            )
            if skip is None
            else (),
            LARGE if skip is None else 16,
        )

    pieces = {}
    grads = []
    for half, (mine, other) in enumerate(halves):
        kept, *packed = call(
            functools.partial(pack_kernel, chips),
            [shape_of((TILE, width), f32)]
            + [shape_of((TILE + PAD, width), i16)] * (chips - 1),
            [VMEM] * 2,
            (mine, other),
            chips * TILE * width * 8,
            chips * TILE * width * 10,
        )
        arrived = [swap(part, "wide", 2 * (k + 1)) for k, part in enumerate(packed)]
        if half == 0:
            kept, here = lax.optimization_barrier((kept, where))
            (held,) = call(
                functools.partial(hold_kernel, held_keys),
                [shape_of((len(held_keys), units, width), bf16)],
                [SMEM, HBM],
                (here, down_weight),
                0,
                len(held_keys) * units * width * 2,
                [pltpu.SemaphoreType.DMA((len(held_keys),))],
                MEDIUM,
            )
            kept, held = lax.optimization_barrier((kept, held))
        (grad,) = call(
            merge_kernel,
            [shape_of((TILE, width), bf16)],
            [VMEM] * chips,
            (kept, *arrived),
            chips * TILE * width * 4,
            chips * TILE * width * 3,
        )
        grads.append(grad)
        for k in range(narrow):
            pieces[k, half] = (swap(grad, "narrow", k),)

    if narrow == 4:
        near_ends = lax.ppermute(grads[0], "narrow", [(1, 2), (2, 1)])
        ends = lax.ppermute(pieces[2, 0][0], "narrow", [(1, 0), (2, 3)])
        pieces[3, 0] = (near_ends, ends)
    early = [(0, half) for half in range(HALVES)] + [(k, 0) for k in range(1, narrow)]
    summed, head_grad = unit(early, "first", None)
    (summed,) = unit(held_keys[:1], "more", 0, summed)
    gate_grad, up_grad = unit(held_keys[1:], "last", 1, summed, gate_pre, up_pre)
    return head_grad, gate_grad, up_grad


def solution(mesh):
    in_specs = (
        P("wide", "narrow"),
        P("wide", "narrow"),
        P(),
        P(),
        P(),
        P(None, "wide", None),
        P(None, "wide"),
        P("wide", "narrow"),
        P("wide", "narrow"),
        P("narrow", None),
    )
    out_specs = (P("wide", "narrow"), P("wide", "narrow"), P("wide", "narrow"))

    return jax.shard_map(
        on_device, mesh=mesh, in_specs=in_specs, out_specs=out_specs, check_vma=False
    )
```

```python
import functools

import jax
import jax.numpy as jnp
from jax import lax
from jax.experimental import pallas as pl
from jax.experimental.pallas import tpu as pltpu
from jax.sharding import PartitionSpec as P


TILE = 128
PAD = 8
GROUPS = 2
HALVES = 2
GROUP_ROWS = 8
AT_ONCE = 24
LARGE = 50
MEDIUM = 46
LEVELS = 32767.0
VMEM = pl.BlockSpec(memory_space=pltpu.VMEM)
SMEM = pl.BlockSpec(memory_space=pltpu.SMEM)
ANY = pl.BlockSpec(memory_space=pl.ANY)
HBM = pl.BlockSpec(memory_space=pltpu.HBM)


def swap(x, axis, mask):
    if mask == 0:
        return x
    size = lax.axis_size(axis)
    return lax.ppermute(x, axis, [(i, i ^ mask) for i in range(size)])


def step_of(code):
    return jnp.exp2(code * 0.125) * (1.0 / LEVELS)


def encode(x):
    peak = jnp.max(jnp.abs(x), axis=0, keepdims=True)
    code = jnp.ceil(8.0 * jnp.log2(jnp.maximum(peak, 1e-30)) + 0.25)
    levels = jnp.round(x * (1.0 / step_of(code)))
    return levels.astype(jnp.int32).astype(jnp.int16), code.astype(jnp.int32)


def decode(levels, code):
    return levels.astype(jnp.int32).astype(jnp.float32) * step_of(code.astype(jnp.float32))


def tiles_kernel(slots, tiles_ref, counts_ref, head, blocks_out, live_out, out, sem):
    blocks, _, per_block = tiles_ref.shape

    def copy(tile, slot):
        return pltpu.make_async_copy(
            head.at[pl.ds(pl.multiple_of(tile * TILE, TILE), TILE), :],
            out.at[pl.ds(pl.multiple_of(slot * TILE, TILE), TILE), :],
            sem.at[slot],
        )

    def place(slot, block, tile):
        blocks_out[slot] = block
        copy(tile, slot).start()

    live = jnp.int32(0)
    for block in range(blocks):
        count = counts_ref[block, 0]
        for j in range(per_block):
            pl.when(j < count)(
                functools.partial(place, live + j, block, tiles_ref[block, 0, j])
            )
        live = live + count
    live_out[0] = live
    for slot in range(slots):
        pl.when(slot >= live)(functools.partial(place, slot, 0, 0))
    for slot in range(slots):
        copy(0, slot).wait()


def logits_kernel(wide, narrow, slots, group, blocks_ref, where_ref, tiles, *refs):
    me_w, me_n = where_ref[0], where_ref[1]
    per = slots // narrow
    share = per // GROUPS
    parts, own, sends = refs[:wide], refs[wide], refs[wide + 1 : wide + narrow]
    rows, sem = refs[wide + narrow :]
    copies = [pltpu.make_async_copy(parts[k], rows.at[k], sem.at[k]) for k in range(wide)]
    for copy in copies:
        copy.start()
    for send in sends:
        send[share * TILE :, :] = jnp.zeros((send.shape[0] - share * TILE, TILE), jnp.int16)
    for copy in copies:
        copy.wait()
    for k in [*range(1, narrow), 0]:
        for i in range(share):
            slot = (me_n ^ k) * per + group * share + i
            part = lax.dot_general(
                rows[blocks_ref[slot] ^ me_w],
                tiles[pl.ds(pl.multiple_of(slot * TILE, TILE), TILE), :],
                (((1,), (1,)), ((), ())),
                preferred_element_type=jnp.float32,
            )
            if k == 0:
                own[i * TILE : (i + 1) * TILE, :] = part
            else:
                levels, code = encode(part)
                sends[k - 1][i * TILE : (i + 1) * TILE, :] = levels
                sends[k - 1][share * TILE + i : share * TILE + i + 1, :] = code.astype(jnp.int16)


def targets_kernel(list_ref, count_ref, code, head, out, groups, more, sem, more_sem):
    blocks = code.shape[0]

    def copy(block, j, buffer, at, sem):
        start = pl.multiple_of(list_ref[block * TILE + j] * GROUP_ROWS, GROUP_ROWS)
        return pltpu.make_async_copy(
            head.at[pl.ds(start, GROUP_ROWS), :],
            buffer.at[pl.ds(pl.multiple_of(at * GROUP_ROWS, GROUP_ROWS), GROUP_ROWS), :],
            sem,
        )

    def place(block, chunk, buffer):
        depth = AT_ONCE * GROUP_ROWS
        wanted = code[block : block + 1, :] - chunk * depth
        spot = lax.broadcasted_iota(jnp.int32, (depth, TILE), 0)
        hit = jnp.where(spot == wanted, 1.0, 0.0).astype(jnp.bfloat16)
        return lax.dot_general(
            hit, buffer[...], (((0,), (0,)), ((), ())), preferred_element_type=jnp.float32
        )

    for block in range(blocks):
        for j in range(AT_ONCE):
            copy(block, j, groups.at[block], j, sem.at[block]).start()
    for block in range(blocks):
        rows = pl.ds(block * TILE, TILE)
        pltpu.make_async_copy(
            head.at[pl.ds(0, AT_ONCE * GROUP_ROWS), :], groups.at[block], sem.at[block]
        ).wait()
        out[rows, :] = place(block, 0, groups.at[block]).astype(jnp.bfloat16)

        @pl.when(count_ref[block] > AT_ONCE)
        def _(block=block, rows=rows):
            def body(chunk, carry):
                def start(j, carry):
                    copy(block, chunk * AT_ONCE + j, more, j, more_sem).start()
                    return carry

                lax.fori_loop(0, AT_ONCE, start, 0)
                pltpu.make_async_copy(
                    head.at[pl.ds(0, AT_ONCE * GROUP_ROWS), :], more, more_sem
                ).wait()
                added = out[rows, :].astype(jnp.float32) + place(block, chunk, more)
                out[rows, :] = added.astype(jnp.bfloat16)
                return carry

            lax.fori_loop(1, (count_ref[block] + AT_ONCE - 1) // AT_ONCE, body, 0)


def probs_kernel(narrow, slots, group, blocks_ref, live_ref, where_ref, own, *refs):
    recvs, lse, weight, out = refs[: narrow - 1], refs[-3], refs[-2], refs[-1]
    per = slots // narrow
    share = per // GROUPS
    codes = [recv[share * TILE :, :] for recv in recvs]
    for i in range(share):
        slot = where_ref[1] * per + group * share + i
        total = own[i * TILE : (i + 1) * TILE, :]
        for recv, code in zip(recvs, codes):
            total = total + decode(recv[i * TILE : (i + 1) * TILE, :], code[i : i + 1, :])
        rows = pl.ds(pl.multiple_of(blocks_ref[slot] * TILE, TILE), TILE)
        scaled = jnp.exp(total - lse[rows, :]) * weight[rows, :]
        out[i * TILE : (i + 1) * TILE, :] = jnp.where(slot < live_ref[0], scaled, 0.0).astype(
            jnp.bfloat16
        )


def grads_kernel(wide, narrow, slots, half, blocks_ref, where_ref, tiles, *refs):
    probs = refs[: narrow * GROUPS]
    target_rows, factor, mine, other, total = refs[narrow * GROUPS :]
    me_w, me_n = where_ref[0], where_ref[1]
    per = slots // narrow
    share = per // GROUPS
    width = mine.shape[1]
    for block in range(factor.shape[0] // TILE):
        rows = slice(block * TILE, (block + 1) * TILE)
        weight = -factor[rows, :]
        for lane in range(0, width, TILE):
            at = half * width + lane
            total[block ^ me_w, :, lane : lane + TILE] = weight * target_rows[
                rows, at : at + TILE
            ].astype(jnp.float32)
    for k in range(narrow):
        for group in range(GROUPS):
            for i in range(share):
                slot = (me_n ^ k) * per + group * share + i
                total[blocks_ref[slot] ^ me_w] += jnp.dot(
                    probs[k * GROUPS + group][i * TILE : (i + 1) * TILE, :],
                    tiles[
                        pl.ds(pl.multiple_of(slot * TILE, TILE), TILE),
                        half * width : (half + 1) * width,
                    ],
                    preferred_element_type=jnp.float32,
                )
    for chip in range(wide // 2):
        mine[chip * TILE : (chip + 1) * TILE, :] = total[2 * chip]
        other[chip * TILE : (chip + 1) * TILE, :] = total[2 * chip + 1]


def pack_kernel(chips, mine, other, own, *sends):
    for chip in [*range(1, chips), 0]:
        rows = slice(chip * TILE, (chip + 1) * TILE)
        if chip == 0:
            own[...] = mine[rows, :] + other[rows, :]
            continue
        send = sends[chip - 1]
        for lane in range(0, own.shape[1], TILE):
            lanes = slice(lane, lane + TILE)
            levels, code = encode(mine[rows, lanes] + other[rows, lanes])
            send[:TILE, lanes] = levels
            send[TILE:, lanes] = jnp.broadcast_to(code, (PAD, TILE)).astype(jnp.int16)


def merge_kernel(own, *refs):
    recvs, out = refs[:-1], refs[-1]
    for lane in range(0, own.shape[1], TILE):
        lanes = slice(lane, lane + TILE)
        total = own[:, lanes]
        for recv in recvs:
            total = total + decode(recv[:TILE, lanes], recv[TILE : TILE + 1, lanes])
        out[:, lanes] = total.astype(jnp.bfloat16)


def down_copies(keys, where_ref, down, out, sem, rows):
    width = out.shape[-1]

    def copy(at):
        mask, half = keys[at]
        start = pl.multiple_of((where_ref[1] ^ mask) * (width * HALVES) + half * width, width)
        return pltpu.make_async_copy(down.at[rows, pl.ds(start, width)], out.at[at], sem.at[at])

    return [copy(at) for at in range(len(keys))]


def hold_kernel(keys, where_ref, down, out, sem):
    copies = down_copies(keys, where_ref, down, out, sem, slice(None))
    for copy in copies:
        copy.start()
    for copy in copies:
        copy.wait()


def unit_kernel(keys, splits, kind, chunk, skip, where_ref, *refs):
    count, inputs = len(keys), sum(splits)
    arrived, down, refs = list(refs[:inputs]), refs[inputs], list(refs[inputs + 1 :])
    units = down.shape[-2]
    width = arrived[0].shape[1]
    pieces = []
    for split in splits:
        piece = arrived.pop(0)[...]
        for _ in range(split - 1):
            piece = piece + arrived.pop(0)[...]
        pieces.append(piece)
    summed = None if kind == "first" else refs.pop(0)
    if kind == "last":
        gate, up, gate_out, up_out = refs[:4]
    else:
        sum_out = refs[0]
    if kind == "first":
        for at in range(HALVES):
            refs[1][:, at * width : (at + 1) * width] = pieces[at]
    steps = [pl.ds(at, chunk) for at in range(0, units, chunk)]
    if skip is None:
        down_v, sem = refs[-2:]
        copies = [
            down_copies(keys, where_ref, down, down_v.at[step], sem.at[step], rows)
            for step, rows in enumerate(steps)
        ]
        for copy in sum(copies, []):
            copy.start()
    for step, rows in enumerate(steps):
        total = None if summed is None else summed[:, rows]
        for at in range(count):
            if skip is None:
                copies[step][at].wait()
            part = lax.dot_general(
                pieces[at],
                down_v[step, at] if skip is None else down[skip + at, rows, :],
                (((1,), (1,)), ((), ())),
                preferred_element_type=jnp.float32,
            )
            total = part if total is None else total + part
        if kind != "last":
            sum_out[:, rows] = total
            continue
        g = gate[:, rows].astype(jnp.float32)
        u = up[:, rows].astype(jnp.float32)
        s = 1.0 / (1.0 + jnp.exp(-g))
        up_out[:, rows] = (total * g * s).astype(jnp.bfloat16)
        gate_out[:, rows] = (total * u * s * (1.0 + g * (1.0 - s))).astype(jnp.bfloat16)


def shape_of(shape, dtype):
    return jax.ShapeDtypeStruct(shape, dtype)


def call(kernel, outs, ins, args, flops, moved, scratch=(), mib=16, scalars=0):
    return pl.pallas_call(
        kernel,
        out_shape=outs,
        in_specs=ins,
        out_specs=[SMEM] * scalars + [VMEM] * (len(outs) - scalars),
        scratch_shapes=list(scratch),
        compiler_params=pltpu.CompilerParams(vmem_limit_bytes=mib * 1024 * 1024),
        cost_estimate=pl.CostEstimate(flops=flops, bytes_accessed=moved, transcendentals=0),
    )(*args)


def on_device(
    hidden,
    head_weight,
    lse,
    targets,
    loss_weight,
    block_tiles,
    block_counts,
    gate_pre,
    up_pre,
    down_weight,
):
    f32, bf16, i16 = jnp.float32, jnp.bfloat16, jnp.int16
    _, features = hidden.shape
    vocab_here = head_weight.shape[0]
    wide, narrow = lax.axis_size("wide"), lax.axis_size("narrow")
    chips = wide // 2
    me_w, me_n = lax.axis_index("wide"), lax.axis_index("narrow")
    where = jnp.stack([me_w, me_n]).astype(jnp.int32)
    blocks, per_block = block_tiles.shape[0], block_tiles.shape[2]
    slots = blocks // 2 * per_block
    share = slots // narrow // GROUPS
    width = features // HALVES

    far = [swap(hidden, "wide", 2 * chip) for chip in range(chips)]

    local_ids = (targets - me_w * vocab_here).reshape(blocks, TILE)
    inside = (local_ids >= 0) & (local_ids < vocab_here)
    order = jnp.arange(TILE, dtype=jnp.int32)
    earlier = (order[None, :] < order[:, None])[None]
    group_ids = jnp.where(inside, local_ids // GROUP_ROWS, -1)
    same = group_ids[:, :, None] == group_ids[:, None, :]
    first = inside & (jnp.sum((same & earlier).astype(jnp.int32), axis=2) == 0)
    rank = jnp.sum((earlier & first[:, None, :]).astype(jnp.int32), axis=2)
    spot = jnp.sum(jnp.where(same & first[:, None, :], rank[:, None, :], 0), axis=2)
    target_code = jnp.where(inside, spot * GROUP_ROWS + local_ids % GROUP_ROWS, -1)
    chosen = first[:, None, :] & (rank[:, None, :] == order[None, :, None])
    target_list = jnp.sum(jnp.where(chosen, group_ids[:, None, :], 0), axis=2)
    target_count = jnp.sum(first.astype(jnp.int32), axis=1)
    spare = jnp.arange(blocks * TILE, dtype=jnp.int32).reshape(blocks, TILE)
    target_list = jnp.where(
        order[None, :] < target_count[:, None],
        target_list,
        spare % (vocab_here // GROUP_ROWS),
    )

    def over_lanes(x):
        return jnp.broadcast_to(x[:, None], (blocks * TILE, TILE))

    lse_rows, weight_rows = over_lanes(lse), over_lanes(loss_weight)
    factor = over_lanes(jnp.where(inside.reshape(-1), loss_weight, 0.0))
    target_list = target_list.reshape(-1)
    counts, where, lse_rows, weight_rows, factor, target_list, target_count, target_code = (
        lax.optimization_barrier(
            (
                *(block_counts, where, lse_rows, weight_rows, factor),
                *(target_list, target_count, target_code),
            )
        )
    )
    slot_blocks, live, tiles = call(
        functools.partial(tiles_kernel, slots),
        [
            shape_of((slots,), jnp.int32),
            shape_of((1,), jnp.int32),
            shape_of((slots * TILE, features), bf16),
        ],
        [SMEM, SMEM, HBM],
        (block_tiles, counts, head_weight),
        0,
        slots * TILE * features * 2,
        [pltpu.SemaphoreType.DMA((slots,))],
        MEDIUM,
        2,
    )
    far[1], tiles = lax.optimization_barrier((far[1], tiles))
    near = [swap(part, "wide", 1) for part in far]
    parts = [part for pair in zip(far, near) for part in pair]

    probs = []
    for group in range(GROUPS):
        result = call(
            functools.partial(logits_kernel, wide, narrow, slots, group),
            [shape_of((share * TILE, TILE), f32)]
            + [shape_of((share * TILE + PAD, TILE), i16)] * (narrow - 1),
            [SMEM] * 2 + [VMEM] + [ANY] * wide,
            (slot_blocks, where, tiles, *parts),
            2 * slots * TILE * TILE * features // GROUPS,
            slots * TILE * features,
            [pltpu.VMEM((wide, TILE, features), bf16), pltpu.SemaphoreType.DMA((wide,))],
        )
        own, *sends = result
        recvs = [swap(send, "narrow", k + 1) for k, send in enumerate(sends)]
        (prob,) = call(
            functools.partial(probs_kernel, narrow, slots, group),
            [shape_of((share * TILE, TILE), bf16)],
            [SMEM] * 3 + [VMEM] * (narrow + 2),
            (slot_blocks, live, where, own, *recvs, lse_rows, weight_rows),
            share * TILE * TILE * 20,
            share * TILE * TILE * 12,
        )
        if group == GROUPS - 1:
            prob, target_code = lax.optimization_barrier((prob, target_code))
        probs.append([swap(prob, "narrow", k) for k in range(narrow)])
    (target_rows,) = call(
        targets_kernel,
        [shape_of((blocks * TILE, features), bf16)],
        [SMEM, SMEM, VMEM, HBM],
        (target_list, target_count, target_code, head_weight),
        2 * blocks * AT_ONCE * GROUP_ROWS * TILE * features,
        blocks * AT_ONCE * GROUP_ROWS * features * 2,
        [
            pltpu.VMEM((blocks, AT_ONCE * GROUP_ROWS, features), bf16),
            pltpu.VMEM((AT_ONCE * GROUP_ROWS, features), bf16),
            pltpu.SemaphoreType.DMA((blocks,)),
            pltpu.SemaphoreType.DMA(()),
        ],
        MEDIUM,
    )
    all_probs = [probs[group][k] for k in range(narrow) for group in range(GROUPS)]

    halves = []
    for half in range(HALVES):
        mine, other = call(
            functools.partial(grads_kernel, wide, narrow, slots, half),
            [shape_of((chips * TILE, width), f32)] * 2,
            [SMEM] * 2 + [VMEM] * (narrow * GROUPS + 3),
            (slot_blocks, where, tiles, *all_probs, target_rows, factor),
            2 * slots * TILE * TILE * width,
            slots * TILE * width * 4,
            [pltpu.VMEM((wide, TILE, width), f32)],
        )
        halves.append((mine, swap(other, "wide", 1)))
    units = gate_pre.shape[1]
    held_keys = [(k, HALVES - 1) for k in range(2, narrow)]
    chunk = units // 2 if units // 2 % TILE == 0 else units

    def unit(keys, kind, skip, *extra):
        last = kind == "last"
        inputs = [part for key in keys for part in pieces[key]]
        count = len(keys)
        return call(
            functools.partial(
                unit_kernel, keys, [len(pieces[key]) for key in keys], kind, chunk, skip
            ),
            [shape_of((TILE, units), bf16)] * 2
            if last
            else [shape_of((TILE, units), f32)]
            + [shape_of((TILE, features), bf16)] * (kind == "first"),
            [SMEM]
            + [VMEM] * len(inputs)
            + [HBM if skip is None else VMEM]
            + [VMEM] * len(extra),
            (where, *inputs, down_weight if skip is None else held, *extra),
            2 * count * TILE * units * width,
            count * units * width * 2,
            (
                pltpu.VMEM((units // chunk, count, chunk, width), bf16),
                pltpu.SemaphoreType.DMA((units // chunk, count)),
            )
            if skip is None
            else (),
            LARGE if skip is None else 16,
        )

    pieces = {}
    grads = []
    for half, (mine, other) in enumerate(halves):
        kept, *packed = call(
            functools.partial(pack_kernel, chips),
            [shape_of((TILE, width), f32)]
            + [shape_of((TILE + PAD, width), i16)] * (chips - 1),
            [VMEM] * 2,
            (mine, other),
            chips * TILE * width * 8,
            chips * TILE * width * 10,
        )
        arrived = [swap(part, "wide", 2 * (k + 1)) for k, part in enumerate(packed)]
        if half == 0:
            kept, here = lax.optimization_barrier((kept, where))
            (held,) = call(
                functools.partial(hold_kernel, held_keys),
                [shape_of((len(held_keys), units, width), bf16)],
                [SMEM, HBM],
                (here, down_weight),
                0,
                len(held_keys) * units * width * 2,
                [pltpu.SemaphoreType.DMA((len(held_keys),))],
                MEDIUM,
            )
            kept, held = lax.optimization_barrier((kept, held))
        (grad,) = call(
            merge_kernel,
            [shape_of((TILE, width), bf16)],
            [VMEM] * chips,
            (kept, *arrived),
            chips * TILE * width * 4,
            chips * TILE * width * 3,
        )
        grads.append(grad)
        for k in range(narrow):
            pieces[k, half] = (swap(grad, "narrow", k),)

    if narrow == 4:
        near_ends = lax.ppermute(grads[0], "narrow", [(1, 2), (2, 1)])
        ends = lax.ppermute(pieces[2, 0][0], "narrow", [(1, 0), (2, 3)])
        pieces[3, 0] = (near_ends, ends)
    early = [(0, half) for half in range(HALVES)] + [(k, 0) for k in range(1, narrow - 1)]
    summed, head_grad = unit(early, "first", None)
    (summed,) = unit([(narrow - 1, 0), (1, 1)], "more", None, summed)
    gate_grad, up_grad = unit(held_keys, "last", 0, summed, gate_pre, up_pre)
    return head_grad, gate_grad, up_grad


def solution(mesh):
    in_specs = (
        P("wide", "narrow"),
        P("wide", "narrow"),
        P(),
        P(),
        P(),
        P(None, "wide", None),
        P(None, "wide"),
        P("wide", "narrow"),
        P("wide", "narrow"),
        P("narrow", None),
    )
    out_specs = (P("wide", "narrow"), P("wide", "narrow"), P("wide", "narrow"))

    return jax.shard_map(
        on_device, mesh=mesh, in_specs=in_specs, out_specs=out_specs, check_vma=False
    )
```

```python
import functools

import jax
import jax.numpy as jnp
from jax import lax
from jax.experimental import pallas as pl
from jax.experimental.pallas import tpu as pltpu
from jax.sharding import PartitionSpec as P


TILE = 128
PAD = 8
GROUPS = 2
HALVES = 2
GROUP_ROWS = 8
AT_ONCE = 24
LARGE = 47
MEDIUM = 46
LEVELS = 32767.0
VMEM = pl.BlockSpec(memory_space=pltpu.VMEM)
SMEM = pl.BlockSpec(memory_space=pltpu.SMEM)
ANY = pl.BlockSpec(memory_space=pl.ANY)
HBM = pl.BlockSpec(memory_space=pltpu.HBM)


def swap(x, axis, mask):
    if mask == 0:
        return x
    size = lax.axis_size(axis)
    return lax.ppermute(x, axis, [(i, i ^ mask) for i in range(size)])


def step_of(code):
    return jnp.exp2(code * 0.125) * (1.0 / LEVELS)


def encode(x):
    peak = jnp.max(jnp.abs(x), axis=0, keepdims=True)
    code = jnp.ceil(8.0 * jnp.log2(jnp.maximum(peak, 1e-30)) + 0.25)
    levels = jnp.round(x * (1.0 / step_of(code)))
    return levels.astype(jnp.int32).astype(jnp.int16), code.astype(jnp.int32)


def decode(levels, code):
    return levels.astype(jnp.int32).astype(jnp.float32) * step_of(code.astype(jnp.float32))


def tiles_kernel(slots, tiles_ref, counts_ref, head, blocks_out, live_out, out, sem):
    blocks, _, per_block = tiles_ref.shape

    def copy(tile, slot):
        return pltpu.make_async_copy(
            head.at[pl.ds(pl.multiple_of(tile * TILE, TILE), TILE), :],
            out.at[pl.ds(pl.multiple_of(slot * TILE, TILE), TILE), :],
            sem.at[slot],
        )

    def place(slot, block, tile):
        blocks_out[slot] = block
        copy(tile, slot).start()

    live = jnp.int32(0)
    for block in range(blocks):
        count = counts_ref[block, 0]
        for j in range(per_block):
            pl.when(j < count)(
                functools.partial(place, live + j, block, tiles_ref[block, 0, j])
            )
        live = live + count
    live_out[0] = live
    for slot in range(slots):
        pl.when(slot >= live)(functools.partial(place, slot, 0, 0))
    for slot in range(slots):
        copy(0, slot).wait()


def logits_kernel(wide, narrow, slots, group, blocks_ref, where_ref, tiles, *refs):
    me_w, me_n = where_ref[0], where_ref[1]
    per = slots // narrow
    share = per // GROUPS
    parts, own, sends = refs[:wide], refs[wide], refs[wide + 1 : wide + narrow]
    rows, sem = refs[wide + narrow :]
    copies = [pltpu.make_async_copy(parts[k], rows.at[k], sem.at[k]) for k in range(wide)]
    for copy in copies:
        copy.start()
    for send in sends:
        send[share * TILE :, :] = jnp.zeros((send.shape[0] - share * TILE, TILE), jnp.int16)
    for copy in copies:
        copy.wait()
    for k in [*range(1, narrow), 0]:
        for i in range(share):
            slot = (me_n ^ k) * per + group * share + i
            part = lax.dot_general(
                rows[blocks_ref[slot] ^ me_w],
                tiles[pl.ds(pl.multiple_of(slot * TILE, TILE), TILE), :],
                (((1,), (1,)), ((), ())),
                preferred_element_type=jnp.float32,
            )
            if k == 0:
                own[i * TILE : (i + 1) * TILE, :] = part
            else:
                levels, code = encode(part)
                sends[k - 1][i * TILE : (i + 1) * TILE, :] = levels
                sends[k - 1][share * TILE + i : share * TILE + i + 1, :] = code.astype(jnp.int16)


def targets_kernel(list_ref, count_ref, code, head, out, groups, more, sem, more_sem):
    blocks = code.shape[0]

    def copy(block, j, buffer, at, sem):
        start = pl.multiple_of(list_ref[block * TILE + j] * GROUP_ROWS, GROUP_ROWS)
        return pltpu.make_async_copy(
            head.at[pl.ds(start, GROUP_ROWS), :],
            buffer.at[pl.ds(pl.multiple_of(at * GROUP_ROWS, GROUP_ROWS), GROUP_ROWS), :],
            sem,
        )

    def place(block, chunk, buffer):
        depth = AT_ONCE * GROUP_ROWS
        wanted = code[block : block + 1, :] - chunk * depth
        spot = lax.broadcasted_iota(jnp.int32, (depth, TILE), 0)
        hit = jnp.where(spot == wanted, 1.0, 0.0).astype(jnp.bfloat16)
        return lax.dot_general(
            hit, buffer[...], (((0,), (0,)), ((), ())), preferred_element_type=jnp.float32
        )

    for block in range(blocks):
        for j in range(AT_ONCE):
            copy(block, j, groups.at[block], j, sem.at[block]).start()
    for block in range(blocks):
        rows = pl.ds(block * TILE, TILE)
        pltpu.make_async_copy(
            head.at[pl.ds(0, AT_ONCE * GROUP_ROWS), :], groups.at[block], sem.at[block]
        ).wait()
        out[rows, :] = place(block, 0, groups.at[block]).astype(jnp.bfloat16)

        @pl.when(count_ref[block] > AT_ONCE)
        def _(block=block, rows=rows):
            def body(chunk, carry):
                def start(j, carry):
                    copy(block, chunk * AT_ONCE + j, more, j, more_sem).start()
                    return carry

                lax.fori_loop(0, AT_ONCE, start, 0)
                pltpu.make_async_copy(
                    head.at[pl.ds(0, AT_ONCE * GROUP_ROWS), :], more, more_sem
                ).wait()
                added = out[rows, :].astype(jnp.float32) + place(block, chunk, more)
                out[rows, :] = added.astype(jnp.bfloat16)
                return carry

            lax.fori_loop(1, (count_ref[block] + AT_ONCE - 1) // AT_ONCE, body, 0)


def probs_kernel(narrow, slots, group, blocks_ref, live_ref, where_ref, own, *refs):
    recvs, lse, weight, out = refs[: narrow - 1], refs[-3], refs[-2], refs[-1]
    per = slots // narrow
    share = per // GROUPS
    codes = [recv[share * TILE :, :] for recv in recvs]
    for i in range(share):
        slot = where_ref[1] * per + group * share + i
        total = own[i * TILE : (i + 1) * TILE, :]
        for recv, code in zip(recvs, codes):
            total = total + decode(recv[i * TILE : (i + 1) * TILE, :], code[i : i + 1, :])
        rows = pl.ds(pl.multiple_of(blocks_ref[slot] * TILE, TILE), TILE)
        scaled = jnp.exp(total - lse[rows, :]) * weight[rows, :]
        out[i * TILE : (i + 1) * TILE, :] = jnp.where(slot < live_ref[0], scaled, 0.0).astype(
            jnp.bfloat16
        )


def add_slots(narrow, slots, group, blocks_ref, where_ref, tiles, probs, total, lanes):
    per = slots // narrow
    share = per // GROUPS
    for k in range(narrow):
        for i in range(share):
            slot = (where_ref[1] ^ k) * per + group * share + i
            block = blocks_ref[slot] ^ where_ref[0]
            rows = pl.ds(pl.multiple_of(block * TILE, TILE), TILE)
            total[rows, :] += jnp.dot(
                probs[k][i * TILE : (i + 1) * TILE, :],
                tiles[pl.ds(pl.multiple_of(slot * TILE, TILE), TILE), lanes],
                preferred_element_type=jnp.float32,
            )


def base_kernel(narrow, slots, blocks_ref, where_ref, tiles, *refs):
    probs, (target_rows, factor, total) = refs[:-3], refs[-3:]
    for block in range(factor.shape[0] // TILE):
        rows = slice(block * TILE, (block + 1) * TILE)
        start = pl.multiple_of((block ^ where_ref[0]) * TILE, TILE)
        weight = -factor[rows, :]
        for lane in range(0, total.shape[1], TILE):
            lanes = slice(lane, lane + TILE)
            total[pl.ds(start, TILE), lanes] = weight * target_rows[rows, lanes].astype(jnp.float32)
    for group in range(GROUPS - 1):
        some = probs[group * narrow : (group + 1) * narrow]
        add_slots(narrow, slots, group, blocks_ref, where_ref, tiles, some, total, slice(None))


def grads_kernel(narrow, slots, half, blocks_ref, where_ref, tiles, *refs):
    probs, (base, mine, other, total) = refs[:-4], refs[-4:]
    width = mine.shape[1]
    lanes = slice(half * width, (half + 1) * width)
    total[...] = base[:, lanes]
    add_slots(narrow, slots, GROUPS - 1, blocks_ref, where_ref, tiles, probs, total, lanes)
    for chip in range(mine.shape[0] // TILE):
        rows = slice(chip * TILE, (chip + 1) * TILE)
        mine[rows, :] = total[2 * chip * TILE : (2 * chip + 1) * TILE, :]
        other[rows, :] = total[(2 * chip + 1) * TILE : (2 * chip + 2) * TILE, :]


def pack_kernel(chips, mine, other, own, *sends):
    for chip in [*range(1, chips), 0]:
        rows = slice(chip * TILE, (chip + 1) * TILE)
        if chip == 0:
            own[...] = mine[rows, :] + other[rows, :]
            continue
        send = sends[chip - 1]
        for lane in range(0, own.shape[1], TILE):
            lanes = slice(lane, lane + TILE)
            levels, code = encode(mine[rows, lanes] + other[rows, lanes])
            send[:TILE, lanes] = levels
            send[TILE:, lanes] = jnp.broadcast_to(code, (PAD, TILE)).astype(jnp.int16)


def merge_kernel(own, *refs):
    recvs, out = refs[:-1], refs[-1]
    for lane in range(0, own.shape[1], TILE):
        lanes = slice(lane, lane + TILE)
        total = own[:, lanes]
        for recv in recvs:
            total = total + decode(recv[:TILE, lanes], recv[TILE : TILE + 1, lanes])
        out[:, lanes] = total.astype(jnp.bfloat16)


def down_copies(keys, where_ref, down, out, sem, rows):
    width = out.shape[-1]

    def copy(at):
        mask, half = keys[at]
        start = pl.multiple_of((where_ref[1] ^ mask) * (width * HALVES) + half * width, width)
        return pltpu.make_async_copy(down.at[rows, pl.ds(start, width)], out.at[at], sem.at[at])

    return [copy(at) for at in range(len(keys))]


def hold_kernel(keys, where_ref, down, out, sem):
    copies = down_copies(keys, where_ref, down, out, sem, slice(None))
    for copy in copies:
        copy.start()
    for copy in copies:
        copy.wait()


def unit_kernel(keys, splits, kind, chunk, ready, where_ref, *refs):
    inputs = sum(splits)
    arrived, down, refs = list(refs[:inputs]), refs[inputs], list(refs[inputs + 1 :])
    units = down.shape[0]
    width = arrived[0].shape[1]
    pieces = []
    for split in splits:
        piece = arrived.pop(0)[...]
        for _ in range(split - 1):
            piece = piece + arrived.pop(0)[...]
        pieces.append(piece)
    held = refs.pop(0) if ready else None
    summed = None if kind == "first" else refs.pop(0)
    if kind == "last":
        gate, up, gate_out, up_out = refs[:4]
    else:
        sum_out = refs[0]
    down_v, sem = refs[-2:]
    steps = [pl.ds(at, chunk) for at in range(0, units, chunk)]
    copies = [
        down_copies(keys[ready:], where_ref, down, down_v.at[step], sem.at[step], rows)
        for step, rows in enumerate(steps)
    ]
    for copy in sum(copies, []):
        copy.start()
    if kind == "first":
        for at in range(HALVES):
            refs[1][:, at * width : (at + 1) * width] = pieces[at]
    for step, rows in enumerate(steps):
        total = None if summed is None else summed[:, rows]
        for at, piece in enumerate(pieces):
            if at >= ready:
                copies[step][at - ready].wait()
            part = lax.dot_general(
                piece,
                held[at, rows, :] if at < ready else down_v[step, at - ready],
                (((1,), (1,)), ((), ())),
                preferred_element_type=jnp.float32,
            )
            total = part if total is None else total + part
        if kind != "last":
            sum_out[:, rows] = total
            continue
        g = gate[:, rows].astype(jnp.float32)
        u = up[:, rows].astype(jnp.float32)
        s = 1.0 / (1.0 + jnp.exp(-g))
        up_out[:, rows] = (total * g * s).astype(jnp.bfloat16)
        gate_out[:, rows] = (total * u * s * (1.0 + g * (1.0 - s))).astype(jnp.bfloat16)


def shape_of(shape, dtype):
    return jax.ShapeDtypeStruct(shape, dtype)


def call(kernel, outs, ins, args, flops, moved, scratch=(), mib=16, scalars=0):
    return pl.pallas_call(
        kernel,
        out_shape=outs,
        in_specs=ins,
        out_specs=[SMEM] * scalars + [VMEM] * (len(outs) - scalars),
        scratch_shapes=list(scratch),
        compiler_params=pltpu.CompilerParams(vmem_limit_bytes=mib * 1024 * 1024),
        cost_estimate=pl.CostEstimate(flops=flops, bytes_accessed=moved, transcendentals=0),
    )(*args)


def on_device(
    hidden,
    head_weight,
    lse,
    targets,
    loss_weight,
    block_tiles,
    block_counts,
    gate_pre,
    up_pre,
    down_weight,
):
    f32, bf16, i16 = jnp.float32, jnp.bfloat16, jnp.int16
    _, features = hidden.shape
    vocab_here = head_weight.shape[0]
    wide, narrow = lax.axis_size("wide"), lax.axis_size("narrow")
    chips = wide // 2
    me_w, me_n = lax.axis_index("wide"), lax.axis_index("narrow")
    where = jnp.stack([me_w, me_n]).astype(jnp.int32)
    blocks, per_block = block_tiles.shape[0], block_tiles.shape[2]
    slots = blocks // 2 * per_block
    share = slots // narrow // GROUPS
    width = features // HALVES

    far = [swap(hidden, "wide", 2 * chip) for chip in range(chips)]

    local_ids = (targets - me_w * vocab_here).reshape(blocks, TILE)
    inside = (local_ids >= 0) & (local_ids < vocab_here)
    order = jnp.arange(TILE, dtype=jnp.int32)
    earlier = (order[None, :] < order[:, None])[None]
    group_ids = jnp.where(inside, local_ids // GROUP_ROWS, -1)
    same = group_ids[:, :, None] == group_ids[:, None, :]
    first = inside & (jnp.sum((same & earlier).astype(jnp.int32), axis=2) == 0)
    rank = jnp.sum((earlier & first[:, None, :]).astype(jnp.int32), axis=2)
    spot = jnp.sum(jnp.where(same & first[:, None, :], rank[:, None, :], 0), axis=2)
    target_code = jnp.where(inside, spot * GROUP_ROWS + local_ids % GROUP_ROWS, -1)
    chosen = first[:, None, :] & (rank[:, None, :] == order[None, :, None])
    target_list = jnp.sum(jnp.where(chosen, group_ids[:, None, :], 0), axis=2)
    target_count = jnp.sum(first.astype(jnp.int32), axis=1)
    spare = jnp.arange(blocks * TILE, dtype=jnp.int32).reshape(blocks, TILE)
    target_list = jnp.where(
        order[None, :] < target_count[:, None],
        target_list,
        spare % (vocab_here // GROUP_ROWS),
    )

    def over_lanes(x):
        return jnp.broadcast_to(x[:, None], (blocks * TILE, TILE))

    lse_rows, weight_rows = over_lanes(lse), over_lanes(loss_weight)
    factor = over_lanes(jnp.where(inside.reshape(-1), loss_weight, 0.0))
    target_list = target_list.reshape(-1)
    counts, where, lse_rows, weight_rows, factor, target_list, target_count, target_code = (
        lax.optimization_barrier(
            (
                *(block_counts, where, lse_rows, weight_rows, factor),
                *(target_list, target_count, target_code),
            )
        )
    )
    slot_blocks, live, tiles = call(
        functools.partial(tiles_kernel, slots),
        [
            shape_of((slots,), jnp.int32),
            shape_of((1,), jnp.int32),
            shape_of((slots * TILE, features), bf16),
        ],
        [SMEM, SMEM, HBM],
        (block_tiles, counts, head_weight),
        0,
        slots * TILE * features * 2,
        [pltpu.SemaphoreType.DMA((slots,))],
        MEDIUM,
        2,
    )
    far[1], tiles = lax.optimization_barrier((far[1], tiles))
    near = [swap(part, "wide", 1) for part in far]
    parts = [part for pair in zip(far, near) for part in pair]

    probs = []
    for group in range(GROUPS):
        result = call(
            functools.partial(logits_kernel, wide, narrow, slots, group),
            [shape_of((share * TILE, TILE), f32)]
            + [shape_of((share * TILE + PAD, TILE), i16)] * (narrow - 1),
            [SMEM] * 2 + [VMEM] + [ANY] * wide,
            (slot_blocks, where, tiles, *parts),
            2 * slots * TILE * TILE * features // GROUPS,
            slots * TILE * features,
            [pltpu.VMEM((wide, TILE, features), bf16), pltpu.SemaphoreType.DMA((wide,))],
        )
        own, *sends = result
        recvs = [swap(send, "narrow", k + 1) for k, send in enumerate(sends)]
        (prob,) = call(
            functools.partial(probs_kernel, narrow, slots, group),
            [shape_of((share * TILE, TILE), bf16)],
            [SMEM] * 3 + [VMEM] * (narrow + 2),
            (slot_blocks, live, where, own, *recvs, lse_rows, weight_rows),
            share * TILE * TILE * 20,
            share * TILE * TILE * 12,
        )
        if group == GROUPS - 1:
            prob, target_code = lax.optimization_barrier((prob, target_code))
        probs.append([swap(prob, "narrow", k) for k in range(narrow)])
    (target_rows,) = call(
        targets_kernel,
        [shape_of((blocks * TILE, features), bf16)],
        [SMEM, SMEM, VMEM, HBM],
        (target_list, target_count, target_code, head_weight),
        2 * blocks * AT_ONCE * GROUP_ROWS * TILE * features,
        blocks * AT_ONCE * GROUP_ROWS * features * 2,
        [
            pltpu.VMEM((blocks, AT_ONCE * GROUP_ROWS, features), bf16),
            pltpu.VMEM((AT_ONCE * GROUP_ROWS, features), bf16),
            pltpu.SemaphoreType.DMA((blocks,)),
            pltpu.SemaphoreType.DMA(()),
        ],
        MEDIUM,
    )
    early_probs = sum(probs[:-1], [])
    (base,) = call(
        functools.partial(base_kernel, narrow, slots),
        [shape_of((blocks * TILE, features), f32)],
        [SMEM] * 2 + [VMEM] * (len(early_probs) + 3),
        (slot_blocks, where, tiles, *early_probs, target_rows, factor),
        slots * TILE * TILE * features,
        blocks * TILE * features * 4,
    )
    probs[-1][-1], base = lax.optimization_barrier((probs[-1][-1], base))

    halves = []
    for half in range(HALVES):
        mine, other = call(
            functools.partial(grads_kernel, narrow, slots, half),
            [shape_of((chips * TILE, width), f32)] * 2,
            [SMEM] * 2 + [VMEM] * (narrow + 2),
            (slot_blocks, where, tiles, *probs[-1], base),
            slots * TILE * TILE * width,
            blocks * TILE * width * 4,
            [pltpu.VMEM((blocks * TILE, width), f32)],
        )
        halves.append((mine, swap(other, "wide", 1)))
    units = gate_pre.shape[1]
    held_keys = [(k, HALVES - 1) for k in range(2, narrow)]
    chunk = units // 2 if units // 2 % TILE == 0 else units

    def unit(keys, kind, ready, *extra):
        last = kind == "last"
        inputs = [part for key in keys for part in pieces[key]]
        count, read = len(keys), len(keys) - ready
        if ready:
            extra = (held, *extra)
        return call(
            functools.partial(
                unit_kernel, keys, [len(pieces[key]) for key in keys], kind, chunk, ready
            ),
            [shape_of((TILE, units), bf16)] * 2
            if last
            else [shape_of((TILE, units), f32)]
            + [shape_of((TILE, features), bf16)] * (kind == "first"),
            [SMEM] + [VMEM] * len(inputs) + [HBM] + [VMEM] * len(extra),
            (where, *inputs, down_weight, *extra),
            2 * count * TILE * units * width,
            count * units * width * 2,
            (
                pltpu.VMEM((units // chunk, read, chunk, width), bf16),
                pltpu.SemaphoreType.DMA((units // chunk, read)),
            ),
            LARGE,
        )

    pieces = {}
    grads = []
    for half, (mine, other) in enumerate(halves):
        kept, *packed = call(
            functools.partial(pack_kernel, chips),
            [shape_of((TILE, width), f32)]
            + [shape_of((TILE + PAD, width), i16)] * (chips - 1),
            [VMEM] * 2,
            (mine, other),
            chips * TILE * width * 8,
            chips * TILE * width * 10,
        )
        arrived = [swap(part, "wide", 2 * (k + 1)) for k, part in enumerate(packed)]
        if half == 0:
            kept, here = lax.optimization_barrier((kept, where))
            (held,) = call(
                functools.partial(hold_kernel, held_keys),
                [shape_of((len(held_keys), units, width), bf16)],
                [SMEM, HBM],
                (here, down_weight),
                0,
                len(held_keys) * units * width * 2,
                [pltpu.SemaphoreType.DMA((len(held_keys),))],
                MEDIUM,
            )
            kept, held = lax.optimization_barrier((kept, held))
        (grad,) = call(
            merge_kernel,
            [shape_of((TILE, width), bf16)],
            [VMEM] * chips,
            (kept, *arrived),
            chips * TILE * width * 4,
            chips * TILE * width * 3,
        )
        grads.append(grad)
        for k in range(narrow):
            pieces[k, half] = (swap(grad, "narrow", k),)

    if narrow == 4:
        near_ends = lax.ppermute(grads[0], "narrow", [(1, 2), (2, 1)])
        ends = lax.ppermute(pieces[2, 0][0], "narrow", [(1, 0), (2, 3)])
        pieces[3, 0] = (near_ends, ends)
    early = [(0, half) for half in range(HALVES)] + [(k, 0) for k in range(1, narrow - 1)]
    summed, head_grad = unit(early, "first", 0)
    (summed,) = unit([(1, 1)], "more", 0, summed)
    gate_grad, up_grad = unit(
        [*held_keys, (narrow - 1, 0)], "last", len(held_keys), summed, gate_pre, up_pre
    )
    return head_grad, gate_grad, up_grad


def solution(mesh):
    in_specs = (
        P("wide", "narrow"),
        P("wide", "narrow"),
        P(),
        P(),
        P(),
        P(None, "wide", None),
        P(None, "wide"),
        P("wide", "narrow"),
        P("wide", "narrow"),
        P("narrow", None),
    )
    out_specs = (P("wide", "narrow"), P("wide", "narrow"), P("wide", "narrow"))

    return jax.shard_map(
        on_device, mesh=mesh, in_specs=in_specs, out_specs=out_specs, check_vma=False
    )
```

```python
import functools

import jax
import jax.numpy as jnp
from jax import lax
from jax.experimental import pallas as pl
from jax.experimental.pallas import tpu as pltpu
from jax.sharding import PartitionSpec as P


TILE = 128
PAD = 8
GROUPS = 2
HALVES = 2
GROUP_ROWS = 8
AT_ONCE = 24
LARGE = 47
MEDIUM = 46
SMALL = 42
LEVELS = 32767.0
VMEM = pl.BlockSpec(memory_space=pltpu.VMEM)
SMEM = pl.BlockSpec(memory_space=pltpu.SMEM)
ANY = pl.BlockSpec(memory_space=pl.ANY)
HBM = pl.BlockSpec(memory_space=pltpu.HBM)


def swap(x, axis, mask):
    if mask == 0:
        return x
    size = lax.axis_size(axis)
    return lax.ppermute(x, axis, [(i, i ^ mask) for i in range(size)])


def step_of(code):
    return jnp.exp2(code * 0.125) * (1.0 / LEVELS)


def encode(x):
    peak = jnp.max(jnp.abs(x), axis=0, keepdims=True)
    code = jnp.ceil(8.0 * jnp.log2(jnp.maximum(peak, 1e-30)) + 0.25)
    levels = jnp.round(x * (1.0 / step_of(code)))
    return levels.astype(jnp.int32).astype(jnp.int16), code.astype(jnp.int32)


def decode(levels, code):
    return levels.astype(jnp.int32).astype(jnp.float32) * step_of(code.astype(jnp.float32))


def tiles_kernel(slots, tiles_ref, counts_ref, head, blocks_out, live_out, out, sem):
    blocks, _, per_block = tiles_ref.shape

    def copy(tile, slot):
        return pltpu.make_async_copy(
            head.at[pl.ds(pl.multiple_of(tile * TILE, TILE), TILE), :],
            out.at[pl.ds(pl.multiple_of(slot * TILE, TILE), TILE), :],
            sem.at[slot],
        )

    def place(slot, block, tile):
        blocks_out[slot] = block
        copy(tile, slot).start()

    live = jnp.int32(0)
    for block in range(blocks):
        count = counts_ref[block, 0]
        for j in range(per_block):
            pl.when(j < count)(
                functools.partial(place, live + j, block, tiles_ref[block, 0, j])
            )
        live = live + count
    live_out[0] = live
    for slot in range(slots):
        pl.when(slot >= live)(functools.partial(place, slot, 0, 0))
    for slot in range(slots):
        copy(0, slot).wait()


def logits_kernel(wide, narrow, slots, group, blocks_ref, where_ref, tiles, *refs):
    me_w, me_n = where_ref[0], where_ref[1]
    per = slots // narrow
    share = per // GROUPS
    parts, own, sends = refs[:wide], refs[wide], refs[wide + 1 : wide + narrow]
    rows, sem = refs[wide + narrow :]
    copies = [pltpu.make_async_copy(parts[k], rows.at[k], sem.at[k]) for k in range(wide)]
    for copy in copies:
        copy.start()
    for send in sends:
        send[share * TILE :, :] = jnp.zeros((send.shape[0] - share * TILE, TILE), jnp.int16)
    for copy in copies:
        copy.wait()
    for k in [*range(1, narrow), 0]:
        for i in range(share):
            slot = (me_n ^ k) * per + group * share + i
            part = lax.dot_general(
                rows[blocks_ref[slot] ^ me_w],
                tiles[pl.ds(pl.multiple_of(slot * TILE, TILE), TILE), :],
                (((1,), (1,)), ((), ())),
                preferred_element_type=jnp.float32,
            )
            if k == 0:
                own[i * TILE : (i + 1) * TILE, :] = part
            else:
                levels, code = encode(part)
                sends[k - 1][i * TILE : (i + 1) * TILE, :] = levels
                sends[k - 1][share * TILE + i : share * TILE + i + 1, :] = code.astype(jnp.int16)


def probs_kernel(narrow, slots, group, blocks_ref, live_ref, where_ref, own, *refs):
    recvs, lse, weight, out = refs[: narrow - 1], refs[-3], refs[-2], refs[-1]
    per = slots // narrow
    share = per // GROUPS
    codes = [recv[share * TILE :, :] for recv in recvs]
    for i in range(share):
        slot = where_ref[1] * per + group * share + i
        total = own[i * TILE : (i + 1) * TILE, :]
        for recv, code in zip(recvs, codes):
            total = total + decode(recv[i * TILE : (i + 1) * TILE, :], code[i : i + 1, :])
        rows = pl.ds(pl.multiple_of(blocks_ref[slot] * TILE, TILE), TILE)
        scaled = jnp.exp(total - lse[rows, :]) * weight[rows, :]
        out[i * TILE : (i + 1) * TILE, :] = jnp.where(slot < live_ref[0], scaled, 0.0).astype(
            jnp.bfloat16
        )


def add_slots(narrow, slots, group, blocks_ref, where_ref, tiles, probs, total, lanes):
    per = slots // narrow
    share = per // GROUPS
    for k in range(narrow):
        for i in range(share):
            slot = (where_ref[1] ^ k) * per + group * share + i
            block = blocks_ref[slot] ^ where_ref[0]
            rows = pl.ds(pl.multiple_of(block * TILE, TILE), TILE)
            total[rows, :] += jnp.dot(
                probs[k][i * TILE : (i + 1) * TILE, :],
                tiles[pl.ds(pl.multiple_of(slot * TILE, TILE), TILE), lanes],
                preferred_element_type=jnp.float32,
            )


def base_kernel(narrow, slots, blocks_ref, where_ref, list_ref, count_ref, head, tiles, *refs):
    probs, (code, factor, total, groups, more, sem, more_sem) = refs[:-7], refs[-7:]
    blocks = code.shape[0]

    def copy(block, j, buffer, at, sem):
        start = pl.multiple_of(list_ref[block * TILE + j] * GROUP_ROWS, GROUP_ROWS)
        return pltpu.make_async_copy(
            head.at[pl.ds(start, GROUP_ROWS), :],
            buffer.at[pl.ds(pl.multiple_of(at * GROUP_ROWS, GROUP_ROWS), GROUP_ROWS), :],
            sem,
        )

    def take(block, chunk, buffer):
        depth = AT_ONCE * GROUP_ROWS
        wanted = code[block : block + 1, :] - chunk * depth
        spot = lax.broadcasted_iota(jnp.int32, (depth, TILE), 0)
        hit = jnp.where(spot == wanted, 1.0, 0.0).astype(jnp.bfloat16)
        found = lax.dot_general(
            hit, buffer[...], (((0,), (0,)), ((), ())), preferred_element_type=jnp.float32
        )
        rows = pl.ds(pl.multiple_of((block ^ where_ref[0]) * TILE, TILE), TILE)
        weight = factor[block * TILE : (block + 1) * TILE, :]
        for lane in range(0, total.shape[1], TILE):
            lanes = slice(lane, lane + TILE)
            total[rows, lanes] -= weight * found[:, lanes]

    for block in range(blocks):
        for j in range(AT_ONCE):
            copy(block, j, groups.at[block], j, sem.at[block]).start()
    total[...] = jnp.zeros_like(total)
    for group in range(GROUPS - 1):
        some = probs[group * narrow : (group + 1) * narrow]
        add_slots(narrow, slots, group, blocks_ref, where_ref, tiles, some, total, slice(None))
    for block in range(blocks):
        pltpu.make_async_copy(
            head.at[pl.ds(0, AT_ONCE * GROUP_ROWS), :], groups.at[block], sem.at[block]
        ).wait()
        take(block, 0, groups.at[block])

        @pl.when(count_ref[block] > AT_ONCE)
        def _(block=block):
            def body(chunk, carry):
                def start(j, carry):
                    copy(block, chunk * AT_ONCE + j, more, j, more_sem).start()
                    return carry

                lax.fori_loop(0, AT_ONCE, start, 0)
                pltpu.make_async_copy(
                    head.at[pl.ds(0, AT_ONCE * GROUP_ROWS), :], more, more_sem
                ).wait()
                take(block, chunk, more)
                return carry

            lax.fori_loop(1, (count_ref[block] + AT_ONCE - 1) // AT_ONCE, body, 0)


def grads_kernel(narrow, slots, half, blocks_ref, where_ref, tiles, *refs):
    probs, (base, mine, other, total) = refs[:-4], refs[-4:]
    width = mine.shape[1]
    lanes = slice(half * width, (half + 1) * width)
    total[...] = base[:, lanes]
    add_slots(narrow, slots, GROUPS - 1, blocks_ref, where_ref, tiles, probs, total, lanes)
    for chip in range(mine.shape[0] // TILE):
        rows = slice(chip * TILE, (chip + 1) * TILE)
        mine[rows, :] = total[2 * chip * TILE : (2 * chip + 1) * TILE, :]
        other[rows, :] = total[(2 * chip + 1) * TILE : (2 * chip + 2) * TILE, :]


def pack_kernel(chips, mine, other, own, *sends):
    for chip in [*range(1, chips), 0]:
        rows = slice(chip * TILE, (chip + 1) * TILE)
        if chip == 0:
            own[...] = mine[rows, :] + other[rows, :]
            continue
        send = sends[chip - 1]
        for lane in range(0, own.shape[1], TILE):
            lanes = slice(lane, lane + TILE)
            levels, code = encode(mine[rows, lanes] + other[rows, lanes])
            send[:TILE, lanes] = levels
            send[TILE:, lanes] = jnp.broadcast_to(code, (PAD, TILE)).astype(jnp.int16)


def merge_kernel(own, *refs):
    recvs, out = refs[:-1], refs[-1]
    for lane in range(0, own.shape[1], TILE):
        lanes = slice(lane, lane + TILE)
        total = own[:, lanes]
        for recv in recvs:
            total = total + decode(recv[:TILE, lanes], recv[TILE : TILE + 1, lanes])
        out[:, lanes] = total.astype(jnp.bfloat16)


def down_copies(keys, where_ref, down, out, sem, rows):
    width = out.shape[-1]

    def copy(at):
        mask, half = keys[at]
        start = pl.multiple_of((where_ref[1] ^ mask) * (width * HALVES) + half * width, width)
        return pltpu.make_async_copy(down.at[rows, pl.ds(start, width)], out.at[at], sem.at[at])

    return [copy(at) for at in range(len(keys))]


def hold_kernel(keys, where_ref, down, out, sem):
    copies = down_copies(keys, where_ref, down, out, sem, slice(None))
    for copy in copies:
        copy.start()
    for copy in copies:
        copy.wait()


def unit_kernel(keys, splits, kind, chunk, ready, keep, where_ref, *refs):
    inputs = sum(splits)
    arrived, down, refs = list(refs[:inputs]), refs[inputs], list(refs[inputs + 1 :])
    units = down.shape[0]
    width = arrived[0].shape[1]
    pieces = []
    for split in splits:
        piece = arrived.pop(0)[...]
        for _ in range(split - 1):
            piece = piece + arrived.pop(0)[...]
        pieces.append(piece)
    held = [refs.pop(0).at[0] for _ in range(ready)]
    summed = None if kind == "first" else refs.pop(0)
    if kind == "last":
        gate, up, gate_out, up_out = refs[:4]
    else:
        sum_out = refs[0]
    down_v, sem, keep_sem = refs[-3:]
    steps = [pl.ds(at, chunk) for at in range(0, units, chunk)]
    copies = [
        down_copies(keys[ready:], where_ref, down, down_v.at[step], sem.at[step], rows)
        for step, rows in enumerate(steps)
    ]
    for copy in sum(copies, []):
        copy.start()
    if keep:
        kept = down_copies(keep, where_ref, down, refs[-4], keep_sem, slice(None))
        for copy in kept:
            copy.start()
    if kind == "first":
        for at in range(HALVES):
            refs[1][:, at * width : (at + 1) * width] = pieces[at]
    for step, rows in enumerate(steps):
        total = None if summed is None else summed[:, rows]
        for at, piece in enumerate(pieces):
            if at >= ready:
                copies[step][at - ready].wait()
            part = lax.dot_general(
                piece,
                held[at][rows, :] if at < ready else down_v[step, at - ready],
                (((1,), (1,)), ((), ())),
                preferred_element_type=jnp.float32,
            )
            total = part if total is None else total + part
        if kind != "last":
            sum_out[:, rows] = total
            continue
        g = gate[:, rows].astype(jnp.float32)
        u = up[:, rows].astype(jnp.float32)
        s = 1.0 / (1.0 + jnp.exp(-g))
        up_out[:, rows] = (total * g * s).astype(jnp.bfloat16)
        gate_out[:, rows] = (total * u * s * (1.0 + g * (1.0 - s))).astype(jnp.bfloat16)
    if keep:
        for copy in kept:
            copy.wait()


def shape_of(shape, dtype):
    return jax.ShapeDtypeStruct(shape, dtype)


def call(kernel, outs, ins, args, flops, moved, scratch=(), mib=16, scalars=0):
    return pl.pallas_call(
        kernel,
        out_shape=outs,
        in_specs=ins,
        out_specs=[SMEM] * scalars + [VMEM] * (len(outs) - scalars),
        scratch_shapes=list(scratch),
        compiler_params=pltpu.CompilerParams(vmem_limit_bytes=mib * 1024 * 1024),
        cost_estimate=pl.CostEstimate(flops=flops, bytes_accessed=moved, transcendentals=0),
    )(*args)


def on_device(
    hidden,
    head_weight,
    lse,
    targets,
    loss_weight,
    block_tiles,
    block_counts,
    gate_pre,
    up_pre,
    down_weight,
):
    f32, bf16, i16 = jnp.float32, jnp.bfloat16, jnp.int16
    _, features = hidden.shape
    vocab_here = head_weight.shape[0]
    wide, narrow = lax.axis_size("wide"), lax.axis_size("narrow")
    chips = wide // 2
    me_w, me_n = lax.axis_index("wide"), lax.axis_index("narrow")
    where = jnp.stack([me_w, me_n]).astype(jnp.int32)
    blocks, per_block = block_tiles.shape[0], block_tiles.shape[2]
    slots = blocks // 2 * per_block
    share = slots // narrow // GROUPS
    width = features // HALVES

    far = [swap(hidden, "wide", 2 * chip) for chip in range(chips)]

    local_ids = (targets - me_w * vocab_here).reshape(blocks, TILE)
    inside = (local_ids >= 0) & (local_ids < vocab_here)
    order = jnp.arange(TILE, dtype=jnp.int32)
    earlier = (order[None, :] < order[:, None])[None]
    group_ids = jnp.where(inside, local_ids // GROUP_ROWS, -1)
    same = group_ids[:, :, None] == group_ids[:, None, :]
    first = inside & (jnp.sum((same & earlier).astype(jnp.int32), axis=2) == 0)
    rank = jnp.sum((earlier & first[:, None, :]).astype(jnp.int32), axis=2)
    spot = jnp.sum(jnp.where(same & first[:, None, :], rank[:, None, :], 0), axis=2)
    target_code = jnp.where(inside, spot * GROUP_ROWS + local_ids % GROUP_ROWS, -1)
    chosen = first[:, None, :] & (rank[:, None, :] == order[None, :, None])
    target_list = jnp.sum(jnp.where(chosen, group_ids[:, None, :], 0), axis=2)
    target_count = jnp.sum(first.astype(jnp.int32), axis=1)
    spare = jnp.arange(blocks * TILE, dtype=jnp.int32).reshape(blocks, TILE)
    target_list = jnp.where(
        order[None, :] < target_count[:, None],
        target_list,
        spare % (vocab_here // GROUP_ROWS),
    )

    def over_lanes(x):
        return jnp.broadcast_to(x[:, None], (blocks * TILE, TILE))

    lse_rows, weight_rows = over_lanes(lse), over_lanes(loss_weight)
    factor = over_lanes(jnp.where(inside.reshape(-1), loss_weight, 0.0))
    target_list = target_list.reshape(-1)
    counts, where, lse_rows, weight_rows, factor, target_list, target_count, target_code = (
        lax.optimization_barrier(
            (
                *(block_counts, where, lse_rows, weight_rows, factor),
                *(target_list, target_count, target_code),
            )
        )
    )
    slot_blocks, live, tiles = call(
        functools.partial(tiles_kernel, slots),
        [
            shape_of((slots,), jnp.int32),
            shape_of((1,), jnp.int32),
            shape_of((slots * TILE, features), bf16),
        ],
        [SMEM, SMEM, HBM],
        (block_tiles, counts, head_weight),
        0,
        slots * TILE * features * 2,
        [pltpu.SemaphoreType.DMA((slots,))],
        MEDIUM,
        2,
    )
    far[1], tiles = lax.optimization_barrier((far[1], tiles))
    near = [swap(part, "wide", 1) for part in far]
    parts = [part for pair in zip(far, near) for part in pair]

    probs = []
    for group in range(GROUPS):
        result = call(
            functools.partial(logits_kernel, wide, narrow, slots, group),
            [shape_of((share * TILE, TILE), f32)]
            + [shape_of((share * TILE + PAD, TILE), i16)] * (narrow - 1),
            [SMEM] * 2 + [VMEM] + [ANY] * wide,
            (slot_blocks, where, tiles, *parts),
            2 * slots * TILE * TILE * features // GROUPS,
            slots * TILE * features,
            [pltpu.VMEM((wide, TILE, features), bf16), pltpu.SemaphoreType.DMA((wide,))],
        )
        own, *sends = result
        recvs = [swap(send, "narrow", k + 1) for k, send in enumerate(sends)]
        (prob,) = call(
            functools.partial(probs_kernel, narrow, slots, group),
            [shape_of((share * TILE, TILE), bf16)],
            [SMEM] * 3 + [VMEM] * (narrow + 2),
            (slot_blocks, live, where, own, *recvs, lse_rows, weight_rows),
            share * TILE * TILE * 20,
            share * TILE * TILE * 12,
        )
        if group == GROUPS - 1:
            prob, target_code = lax.optimization_barrier((prob, target_code))
        probs.append([swap(prob, "narrow", k) for k in range(narrow)])
    early_probs = sum(probs[:-1], [])
    (base,) = call(
        functools.partial(base_kernel, narrow, slots),
        [shape_of((blocks * TILE, features), f32)],
        [SMEM] * 4 + [HBM] + [VMEM] * (len(early_probs) + 3),
        (
            *(slot_blocks, where, target_list, target_count, head_weight),
            *(tiles, *early_probs, target_code, factor),
        ),
        2 * blocks * AT_ONCE * GROUP_ROWS * TILE * features,
        blocks * TILE * features * 8,
        [
            pltpu.VMEM((blocks, AT_ONCE * GROUP_ROWS, features), bf16),
            pltpu.VMEM((AT_ONCE * GROUP_ROWS, features), bf16),
            pltpu.SemaphoreType.DMA((blocks,)),
            pltpu.SemaphoreType.DMA(()),
        ],
        SMALL,
    )
    probs[-1][-1], base = lax.optimization_barrier((probs[-1][-1], base))

    halves = []
    for half in range(HALVES):
        mine, other = call(
            functools.partial(grads_kernel, narrow, slots, half),
            [shape_of((chips * TILE, width), f32)] * 2,
            [SMEM] * 2 + [VMEM] * (narrow + 2),
            (slot_blocks, where, tiles, *probs[-1], base),
            slots * TILE * TILE * width,
            blocks * TILE * width * 4,
            [pltpu.VMEM((blocks * TILE, width), f32)],
        )
        halves.append((mine, swap(other, "wide", 1)))
    units = gate_pre.shape[1]
    last_keys = [(k, HALVES - 1) for k in range(2, narrow)]
    held_keys = last_keys[:1]
    chunk = units // 2 if units // 2 % TILE == 0 else units

    def unit(keys, kind, held, keep, *extra):
        last = kind == "last"
        inputs = [part for key in keys for part in pieces[key]]
        count, read = len(keys), len(keys) - len(held)
        extra = (*held, *extra)
        return call(
            functools.partial(
                *(unit_kernel, keys, [len(pieces[key]) for key in keys], kind, chunk),
                *(len(held), keep),
            ),
            [shape_of((TILE, units), bf16)] * 2
            if last
            else [shape_of((TILE, units), f32)]
            + [shape_of((TILE, features), bf16)] * (kind == "first")
            + [shape_of((len(keep), units, width), bf16)] * bool(keep),
            [SMEM] + [VMEM] * len(inputs) + [HBM] + [VMEM] * len(extra),
            (where, *inputs, down_weight, *extra),
            2 * count * TILE * units * width,
            count * units * width * 2,
            (
                pltpu.VMEM((units // chunk, read, chunk, width), bf16),
                pltpu.SemaphoreType.DMA((units // chunk, read)),
                pltpu.SemaphoreType.DMA((max(1, len(keep)),)),
            ),
            LARGE,
        )

    pieces = {}
    grads = []
    for half, (mine, other) in enumerate(halves):
        kept, *packed = call(
            functools.partial(pack_kernel, chips),
            [shape_of((TILE, width), f32)]
            + [shape_of((TILE + PAD, width), i16)] * (chips - 1),
            [VMEM] * 2,
            (mine, other),
            chips * TILE * width * 8,
            chips * TILE * width * 10,
        )
        arrived = [swap(part, "wide", 2 * (k + 1)) for k, part in enumerate(packed)]
        if half == 0:
            kept, here = lax.optimization_barrier((kept, where))
            (held,) = call(
                functools.partial(hold_kernel, held_keys),
                [shape_of((len(held_keys), units, width), bf16)],
                [SMEM, HBM],
                (here, down_weight),
                0,
                len(held_keys) * units * width * 2,
                [pltpu.SemaphoreType.DMA((len(held_keys),))],
                MEDIUM,
            )
            kept, held = lax.optimization_barrier((kept, held))
        (grad,) = call(
            merge_kernel,
            [shape_of((TILE, width), bf16)],
            [VMEM] * chips,
            (kept, *arrived),
            chips * TILE * width * 4,
            chips * TILE * width * 3,
        )
        grads.append(grad)
        for k in range(narrow):
            pieces[k, half] = (swap(grad, "narrow", k),)

    if narrow == 4:
        near_ends = lax.ppermute(grads[0], "narrow", [(1, 2), (2, 1)])
        ends = lax.ppermute(pieces[2, 0][0], "narrow", [(1, 0), (2, 3)])
        pieces[3, 0] = (near_ends, ends)
    early = [(0, half) for half in range(HALVES)] + [(k, 0) for k in range(1, narrow - 1)]
    summed, head_grad = unit(early, "first", [], [])
    summed, kept = unit([(1, 1)], "more", [], last_keys[1:2], summed)
    gate_grad, up_grad = unit(
        *([*last_keys, (narrow - 1, 0)], "last", [held, kept], []),
        *(summed, gate_pre, up_pre),
    )
    return head_grad, gate_grad, up_grad


def solution(mesh):
    in_specs = (
        P("wide", "narrow"),
        P("wide", "narrow"),
        P(),
        P(),
        P(),
        P(None, "wide", None),
        P(None, "wide"),
        P("wide", "narrow"),
        P("wide", "narrow"),
        P("narrow", None),
    )
    out_specs = (P("wide", "narrow"), P("wide", "narrow"), P("wide", "narrow"))

    return jax.shard_map(
        on_device, mesh=mesh, in_specs=in_specs, out_specs=out_specs, check_vma=False
    )
```

```python
import functools

import jax
import jax.numpy as jnp
from jax import lax
from jax.experimental import pallas as pl
from jax.experimental.pallas import tpu as pltpu
from jax.sharding import PartitionSpec as P


TILE = 128
PAD = 8
GROUPS = 2
HALVES = 2
GROUP_ROWS = 8
AT_ONCE = 24
LARGE = 47
MEDIUM = 46
LEVELS = 32767.0
VMEM = pl.BlockSpec(memory_space=pltpu.VMEM)
SMEM = pl.BlockSpec(memory_space=pltpu.SMEM)
ANY = pl.BlockSpec(memory_space=pl.ANY)
HBM = pl.BlockSpec(memory_space=pltpu.HBM)


def swap(x, axis, mask):
    if mask == 0:
        return x
    size = lax.axis_size(axis)
    return lax.ppermute(x, axis, [(i, i ^ mask) for i in range(size)])


def step_of(code):
    return jnp.exp2(code * 0.125) * (1.0 / LEVELS)


def encode(x):
    peak = jnp.max(jnp.abs(x), axis=0, keepdims=True)
    code = jnp.ceil(8.0 * jnp.log2(jnp.maximum(peak, 1e-30)) + 0.25)
    levels = jnp.round(x * (1.0 / step_of(code)))
    return levels.astype(jnp.int32).astype(jnp.int16), code.astype(jnp.int32)


def decode(levels, code):
    return levels.astype(jnp.int32).astype(jnp.float32) * step_of(code.astype(jnp.float32))


def tiles_kernel(slots, tiles_ref, counts_ref, head, blocks_out, live_out, out, sem):
    blocks, _, per_block = tiles_ref.shape

    def copy(tile, slot):
        return pltpu.make_async_copy(
            head.at[pl.ds(pl.multiple_of(tile * TILE, TILE), TILE), :],
            out.at[pl.ds(pl.multiple_of(slot * TILE, TILE), TILE), :],
            sem.at[slot],
        )

    def place(slot, block, tile):
        blocks_out[slot] = block
        copy(tile, slot).start()

    live = jnp.int32(0)
    for block in range(blocks):
        count = counts_ref[block, 0]
        for j in range(per_block):
            pl.when(j < count)(
                functools.partial(place, live + j, block, tiles_ref[block, 0, j])
            )
        live = live + count
    live_out[0] = live
    for slot in range(slots):
        pl.when(slot >= live)(functools.partial(place, slot, 0, 0))
    for slot in range(slots):
        copy(0, slot).wait()


def logits_kernel(wide, narrow, slots, group, blocks_ref, where_ref, tiles, *refs):
    me_w, me_n = where_ref[0], where_ref[1]
    per = slots // narrow
    share = per // GROUPS
    parts, own, sends = refs[:wide], refs[wide], refs[wide + 1 : wide + narrow]
    rows, sem = refs[wide + narrow :]
    copies = [pltpu.make_async_copy(parts[k], rows.at[k], sem.at[k]) for k in range(wide)]
    for copy in copies:
        copy.start()
    for send in sends:
        send[share * TILE :, :] = jnp.zeros((send.shape[0] - share * TILE, TILE), jnp.int16)
    for copy in copies:
        copy.wait()
    for k in [*range(1, narrow), 0]:
        for i in range(share):
            slot = (me_n ^ k) * per + group * share + i
            part = lax.dot_general(
                rows[blocks_ref[slot] ^ me_w],
                tiles[pl.ds(pl.multiple_of(slot * TILE, TILE), TILE), :],
                (((1,), (1,)), ((), ())),
                preferred_element_type=jnp.float32,
            )
            if k == 0:
                own[i * TILE : (i + 1) * TILE, :] = part
            else:
                levels, code = encode(part)
                sends[k - 1][i * TILE : (i + 1) * TILE, :] = levels
                sends[k - 1][share * TILE + i : share * TILE + i + 1, :] = code.astype(jnp.int16)


def targets_kernel(list_ref, count_ref, code, head, out, groups, more, sem, more_sem):
    blocks = code.shape[0]

    def copy(block, j, buffer, at, sem):
        start = pl.multiple_of(list_ref[block * TILE + j] * GROUP_ROWS, GROUP_ROWS)
        return pltpu.make_async_copy(
            head.at[pl.ds(start, GROUP_ROWS), :],
            buffer.at[pl.ds(pl.multiple_of(at * GROUP_ROWS, GROUP_ROWS), GROUP_ROWS), :],
            sem,
        )

    def place(block, chunk, buffer):
        depth = AT_ONCE * GROUP_ROWS
        wanted = code[block : block + 1, :] - chunk * depth
        spot = lax.broadcasted_iota(jnp.int32, (depth, TILE), 0)
        hit = jnp.where(spot == wanted, 1.0, 0.0).astype(jnp.bfloat16)
        return lax.dot_general(
            hit, buffer[...], (((0,), (0,)), ((), ())), preferred_element_type=jnp.float32
        )

    for block in range(blocks):
        for j in range(AT_ONCE):
            copy(block, j, groups.at[block], j, sem.at[block]).start()
    for block in range(blocks):
        rows = pl.ds(block * TILE, TILE)
        pltpu.make_async_copy(
            head.at[pl.ds(0, AT_ONCE * GROUP_ROWS), :], groups.at[block], sem.at[block]
        ).wait()
        out[rows, :] = place(block, 0, groups.at[block]).astype(jnp.bfloat16)

        @pl.when(count_ref[block] > AT_ONCE)
        def _(block=block, rows=rows):
            def body(chunk, carry):
                def start(j, carry):
                    copy(block, chunk * AT_ONCE + j, more, j, more_sem).start()
                    return carry

                lax.fori_loop(0, AT_ONCE, start, 0)
                pltpu.make_async_copy(
                    head.at[pl.ds(0, AT_ONCE * GROUP_ROWS), :], more, more_sem
                ).wait()
                added = out[rows, :].astype(jnp.float32) + place(block, chunk, more)
                out[rows, :] = added.astype(jnp.bfloat16)
                return carry

            lax.fori_loop(1, (count_ref[block] + AT_ONCE - 1) // AT_ONCE, body, 0)


def probs_kernel(narrow, slots, group, blocks_ref, live_ref, where_ref, own, *refs):
    recvs, lse, weight, out = refs[: narrow - 1], refs[-3], refs[-2], refs[-1]
    per = slots // narrow
    share = per // GROUPS
    codes = [recv[share * TILE :, :] for recv in recvs]
    for i in range(share):
        slot = where_ref[1] * per + group * share + i
        total = own[i * TILE : (i + 1) * TILE, :]
        for recv, code in zip(recvs, codes):
            total = total + decode(recv[i * TILE : (i + 1) * TILE, :], code[i : i + 1, :])
        rows = pl.ds(pl.multiple_of(blocks_ref[slot] * TILE, TILE), TILE)
        scaled = jnp.exp(total - lse[rows, :]) * weight[rows, :]
        out[i * TILE : (i + 1) * TILE, :] = jnp.where(slot < live_ref[0], scaled, 0.0).astype(
            jnp.bfloat16
        )


def add_slots(narrow, slots, group, blocks_ref, where_ref, tiles, probs, total, lanes):
    per = slots // narrow
    share = per // GROUPS
    for k in range(narrow):
        for i in range(share):
            slot = (where_ref[1] ^ k) * per + group * share + i
            block = blocks_ref[slot] ^ where_ref[0]
            rows = pl.ds(pl.multiple_of(block * TILE, TILE), TILE)
            total[rows, :] += jnp.dot(
                probs[k][i * TILE : (i + 1) * TILE, :],
                tiles[pl.ds(pl.multiple_of(slot * TILE, TILE), TILE), lanes],
                preferred_element_type=jnp.float32,
            )


def base_kernel(narrow, slots, blocks_ref, where_ref, tiles, *refs):
    probs, (target_rows, factor, total) = refs[:-3], refs[-3:]
    for block in range(factor.shape[0] // TILE):
        rows = slice(block * TILE, (block + 1) * TILE)
        start = pl.multiple_of((block ^ where_ref[0]) * TILE, TILE)
        weight = -factor[rows, :]
        for lane in range(0, total.shape[1], TILE):
            lanes = slice(lane, lane + TILE)
            total[pl.ds(start, TILE), lanes] = weight * target_rows[rows, lanes].astype(jnp.float32)
    for group in range(GROUPS - 1):
        some = probs[group * narrow : (group + 1) * narrow]
        add_slots(narrow, slots, group, blocks_ref, where_ref, tiles, some, total, slice(None))


def grads_kernel(narrow, slots, half, blocks_ref, where_ref, tiles, *refs):
    probs, (base, mine, other, total) = refs[:-4], refs[-4:]
    width = mine.shape[1]
    lanes = slice(half * width, (half + 1) * width)
    total[...] = base[:, lanes]
    add_slots(narrow, slots, GROUPS - 1, blocks_ref, where_ref, tiles, probs, total, lanes)
    for chip in range(mine.shape[0] // TILE):
        rows = slice(chip * TILE, (chip + 1) * TILE)
        mine[rows, :] = total[2 * chip * TILE : (2 * chip + 1) * TILE, :]
        other[rows, :] = total[(2 * chip + 1) * TILE : (2 * chip + 2) * TILE, :]


def pack_kernel(chips, mine, other, own, *sends):
    for chip in [*range(1, chips), 0]:
        rows = slice(chip * TILE, (chip + 1) * TILE)
        if chip == 0:
            own[...] = mine[rows, :] + other[rows, :]
            continue
        send = sends[chip - 1]
        for lane in range(0, own.shape[1], TILE):
            lanes = slice(lane, lane + TILE)
            levels, code = encode(mine[rows, lanes] + other[rows, lanes])
            send[:TILE, lanes] = levels
            send[TILE:, lanes] = jnp.broadcast_to(code, (PAD, TILE)).astype(jnp.int16)


def merge_kernel(own, *refs):
    recvs, out = refs[:-1], refs[-1]
    for lane in range(0, own.shape[1], TILE):
        lanes = slice(lane, lane + TILE)
        total = own[:, lanes]
        for recv in recvs:
            total = total + decode(recv[:TILE, lanes], recv[TILE : TILE + 1, lanes])
        out[:, lanes] = total.astype(jnp.bfloat16)


def down_copies(keys, where_ref, down, out, sem, rows):
    width = out.shape[-1]

    def copy(at):
        mask, half = keys[at]
        start = pl.multiple_of((where_ref[1] ^ mask) * (width * HALVES) + half * width, width)
        return pltpu.make_async_copy(down.at[rows, pl.ds(start, width)], out.at[at], sem.at[at])

    return [copy(at) for at in range(len(keys))]


def hold_kernel(keys, chunk, where_ref, down, out, read, sem):
    units, width = down.shape[0], out.shape[1]
    steps = range(0, units, chunk)
    copies = [
        down_copies(keys, where_ref, down, read.at[step], sem.at[step], pl.ds(at, chunk))
        for step, at in enumerate(steps)
    ]
    for at in range(len(keys)):
        for some in copies:
            some[at].start()
    for at in range(len(keys)):
        for step, start in enumerate(steps):
            copies[step][at].wait()
            for row in range(0, chunk, TILE):
                for lane in range(0, width, TILE):
                    out[at, lane : lane + TILE, start + row : start + row + TILE] = read[
                        step, at, row : row + TILE, lane : lane + TILE
                    ].T


def unit_kernel(keys, splits, kind, chunk, ready, where_ref, *refs):
    inputs = sum(splits)
    arrived, down, refs = list(refs[:inputs]), refs[inputs], list(refs[inputs + 1 :])
    units = down.shape[0]
    width = arrived[0].shape[1]
    pieces = []
    for split in splits:
        piece = arrived.pop(0)[...]
        for _ in range(split - 1):
            piece = piece + arrived.pop(0)[...]
        pieces.append(piece)
    held = refs.pop(0) if ready else None
    summed = None if kind == "first" else refs.pop(0)
    if kind == "last":
        gate, up, gate_out, up_out = refs[:4]
    else:
        sum_out = refs[0]
    down_v, sem = refs[-2:]
    steps = [pl.ds(at, chunk) for at in range(0, units, chunk)]
    copies = [
        down_copies(keys[ready:], where_ref, down, down_v.at[step], sem.at[step], rows)
        for step, rows in enumerate(steps)
    ]
    for copy in sum(copies, []):
        copy.start()
    if kind == "first":
        for at in range(HALVES):
            refs[1][:, at * width : (at + 1) * width] = pieces[at]
    for step, rows in enumerate(steps):
        total = None if summed is None else summed[:, rows]
        for at, piece in enumerate(pieces):
            if at >= ready:
                copies[step][at - ready].wait()
            part = lax.dot_general(
                piece,
                held[at, :, rows] if at < ready else down_v[step, at - ready],
                (((1,), (0 if at < ready else 1,)), ((), ())),
                preferred_element_type=jnp.float32,
            )
            total = part if total is None else total + part
        if kind != "last":
            sum_out[:, rows] = total
            continue
        g = gate[:, rows].astype(jnp.float32)
        u = up[:, rows].astype(jnp.float32)
        s = 1.0 / (1.0 + jnp.exp(-g))
        up_out[:, rows] = (total * g * s).astype(jnp.bfloat16)
        gate_out[:, rows] = (total * u * s * (1.0 + g * (1.0 - s))).astype(jnp.bfloat16)


def shape_of(shape, dtype):
    return jax.ShapeDtypeStruct(shape, dtype)


def call(kernel, outs, ins, args, flops, moved, scratch=(), mib=16, scalars=0):
    return pl.pallas_call(
        kernel,
        out_shape=outs,
        in_specs=ins,
        out_specs=[SMEM] * scalars + [VMEM] * (len(outs) - scalars),
        scratch_shapes=list(scratch),
        compiler_params=pltpu.CompilerParams(vmem_limit_bytes=mib * 1024 * 1024),
        cost_estimate=pl.CostEstimate(flops=flops, bytes_accessed=moved, transcendentals=0),
    )(*args)


def on_device(
    hidden,
    head_weight,
    lse,
    targets,
    loss_weight,
    block_tiles,
    block_counts,
    gate_pre,
    up_pre,
    down_weight,
):
    f32, bf16, i16 = jnp.float32, jnp.bfloat16, jnp.int16
    _, features = hidden.shape
    vocab_here = head_weight.shape[0]
    wide, narrow = lax.axis_size("wide"), lax.axis_size("narrow")
    chips = wide // 2
    me_w, me_n = lax.axis_index("wide"), lax.axis_index("narrow")
    where = jnp.stack([me_w, me_n]).astype(jnp.int32)
    blocks, per_block = block_tiles.shape[0], block_tiles.shape[2]
    slots = blocks // 2 * per_block
    share = slots // narrow // GROUPS
    width = features // HALVES

    far = [swap(hidden, "wide", 2 * chip) for chip in range(chips)]

    local_ids = (targets - me_w * vocab_here).reshape(blocks, TILE)
    inside = (local_ids >= 0) & (local_ids < vocab_here)
    order = jnp.arange(TILE, dtype=jnp.int32)
    earlier = (order[None, :] < order[:, None])[None]
    group_ids = jnp.where(inside, local_ids // GROUP_ROWS, -1)
    same = group_ids[:, :, None] == group_ids[:, None, :]
    first = inside & (jnp.sum((same & earlier).astype(jnp.int32), axis=2) == 0)
    rank = jnp.sum((earlier & first[:, None, :]).astype(jnp.int32), axis=2)
    spot = jnp.sum(jnp.where(same & first[:, None, :], rank[:, None, :], 0), axis=2)
    target_code = jnp.where(inside, spot * GROUP_ROWS + local_ids % GROUP_ROWS, -1)
    chosen = first[:, None, :] & (rank[:, None, :] == order[None, :, None])
    target_list = jnp.sum(jnp.where(chosen, group_ids[:, None, :], 0), axis=2)
    target_count = jnp.sum(first.astype(jnp.int32), axis=1)
    spare = jnp.arange(blocks * TILE, dtype=jnp.int32).reshape(blocks, TILE)
    target_list = jnp.where(
        order[None, :] < target_count[:, None],
        target_list,
        spare % (vocab_here // GROUP_ROWS),
    )

    def over_lanes(x):
        return jnp.broadcast_to(x[:, None], (blocks * TILE, TILE))

    lse_rows, weight_rows = over_lanes(lse), over_lanes(loss_weight)
    factor = over_lanes(jnp.where(inside.reshape(-1), loss_weight, 0.0))
    target_list = target_list.reshape(-1)
    counts, where, lse_rows, weight_rows, factor, target_list, target_count, target_code = (
        lax.optimization_barrier(
            (
                *(block_counts, where, lse_rows, weight_rows, factor),
                *(target_list, target_count, target_code),
            )
        )
    )
    slot_blocks, live, tiles = call(
        functools.partial(tiles_kernel, slots),
        [
            shape_of((slots,), jnp.int32),
            shape_of((1,), jnp.int32),
            shape_of((slots * TILE, features), bf16),
        ],
        [SMEM, SMEM, HBM],
        (block_tiles, counts, head_weight),
        0,
        slots * TILE * features * 2,
        [pltpu.SemaphoreType.DMA((slots,))],
        MEDIUM,
        2,
    )
    far[1], tiles = lax.optimization_barrier((far[1], tiles))
    near = [swap(part, "wide", 1) for part in far]
    parts = [part for pair in zip(far, near) for part in pair]

    probs = []
    for group in range(GROUPS):
        result = call(
            functools.partial(logits_kernel, wide, narrow, slots, group),
            [shape_of((share * TILE, TILE), f32)]
            + [shape_of((share * TILE + PAD, TILE), i16)] * (narrow - 1),
            [SMEM] * 2 + [VMEM] + [ANY] * wide,
            (slot_blocks, where, tiles, *parts),
            2 * slots * TILE * TILE * features // GROUPS,
            slots * TILE * features,
            [pltpu.VMEM((wide, TILE, features), bf16), pltpu.SemaphoreType.DMA((wide,))],
        )
        own, *sends = result
        recvs = [swap(send, "narrow", k + 1) for k, send in enumerate(sends)]
        (prob,) = call(
            functools.partial(probs_kernel, narrow, slots, group),
            [shape_of((share * TILE, TILE), bf16)],
            [SMEM] * 3 + [VMEM] * (narrow + 2),
            (slot_blocks, live, where, own, *recvs, lse_rows, weight_rows),
            share * TILE * TILE * 20,
            share * TILE * TILE * 12,
        )
        if group == GROUPS - 1:
            prob, target_code = lax.optimization_barrier((prob, target_code))
        probs.append([swap(prob, "narrow", k) for k in range(narrow)])
    (target_rows,) = call(
        targets_kernel,
        [shape_of((blocks * TILE, features), bf16)],
        [SMEM, SMEM, VMEM, HBM],
        (target_list, target_count, target_code, head_weight),
        2 * blocks * AT_ONCE * GROUP_ROWS * TILE * features,
        blocks * AT_ONCE * GROUP_ROWS * features * 2,
        [
            pltpu.VMEM((blocks, AT_ONCE * GROUP_ROWS, features), bf16),
            pltpu.VMEM((AT_ONCE * GROUP_ROWS, features), bf16),
            pltpu.SemaphoreType.DMA((blocks,)),
            pltpu.SemaphoreType.DMA(()),
        ],
        MEDIUM,
    )
    early_probs = sum(probs[:-1], [])
    (base,) = call(
        functools.partial(base_kernel, narrow, slots),
        [shape_of((blocks * TILE, features), f32)],
        [SMEM] * 2 + [VMEM] * (len(early_probs) + 3),
        (slot_blocks, where, tiles, *early_probs, target_rows, factor),
        slots * TILE * TILE * features,
        blocks * TILE * features * 4,
    )
    probs[-1][-1], base = lax.optimization_barrier((probs[-1][-1], base))

    halves = []
    for half in range(HALVES):
        mine, other = call(
            functools.partial(grads_kernel, narrow, slots, half),
            [shape_of((chips * TILE, width), f32)] * 2,
            [SMEM] * 2 + [VMEM] * (narrow + 2),
            (slot_blocks, where, tiles, *probs[-1], base),
            slots * TILE * TILE * width,
            blocks * TILE * width * 4,
            [pltpu.VMEM((blocks * TILE, width), f32)],
        )
        halves.append((mine, swap(other, "wide", 1)))
    units = gate_pre.shape[1]
    held_keys = [(k, HALVES - 1) for k in range(2, narrow)]
    chunk = units // 2 if units // 2 % TILE == 0 else units

    def unit(keys, kind, ready, *extra):
        last = kind == "last"
        inputs = [part for key in keys for part in pieces[key]]
        count, read = len(keys), len(keys) - ready
        if ready:
            extra = (held, *extra)
        return call(
            functools.partial(
                unit_kernel, keys, [len(pieces[key]) for key in keys], kind, chunk, ready
            ),
            [shape_of((TILE, units), bf16)] * 2
            if last
            else [shape_of((TILE, units), f32)]
            + [shape_of((TILE, features), bf16)] * (kind == "first"),
            [SMEM] + [VMEM] * len(inputs) + [HBM] + [VMEM] * len(extra),
            (where, *inputs, down_weight, *extra),
            2 * count * TILE * units * width,
            count * units * width * 2,
            (
                pltpu.VMEM((units // chunk, read, chunk, width), bf16),
                pltpu.SemaphoreType.DMA((units // chunk, read)),
            ),
            LARGE,
        )

    pieces = {}
    grads = []
    for half, (mine, other) in enumerate(halves):
        kept, *packed = call(
            functools.partial(pack_kernel, chips),
            [shape_of((TILE, width), f32)]
            + [shape_of((TILE + PAD, width), i16)] * (chips - 1),
            [VMEM] * 2,
            (mine, other),
            chips * TILE * width * 8,
            chips * TILE * width * 10,
        )
        arrived = [swap(part, "wide", 2 * (k + 1)) for k, part in enumerate(packed)]
        if half == 0:
            kept, here = lax.optimization_barrier((kept, where))
            (held,) = call(
                functools.partial(hold_kernel, held_keys, chunk),
                [shape_of((len(held_keys), width, units), bf16)],
                [SMEM, HBM],
                (here, down_weight),
                0,
                len(held_keys) * units * width * 2,
                [
                    pltpu.VMEM((units // chunk, len(held_keys), chunk, width), bf16),
                    pltpu.SemaphoreType.DMA((units // chunk, len(held_keys))),
                ],
                MEDIUM,
            )
            kept, held = lax.optimization_barrier((kept, held))
        (grad,) = call(
            merge_kernel,
            [shape_of((TILE, width), bf16)],
            [VMEM] * chips,
            (kept, *arrived),
            chips * TILE * width * 4,
            chips * TILE * width * 3,
        )
        grads.append(grad)
        for k in range(narrow):
            pieces[k, half] = (swap(grad, "narrow", k),)

    if narrow == 4:
        near_ends = lax.ppermute(grads[0], "narrow", [(1, 2), (2, 1)])
        ends = lax.ppermute(pieces[2, 0][0], "narrow", [(1, 0), (2, 3)])
        pieces[3, 0] = (near_ends, ends)
    early = [(0, half) for half in range(HALVES)] + [(k, 0) for k in range(1, narrow - 1)]
    summed, head_grad = unit(early, "first", 0)
    (summed,) = unit([(1, 1)], "more", 0, summed)
    gate_grad, up_grad = unit(
        [*held_keys, (narrow - 1, 0)], "last", len(held_keys), summed, gate_pre, up_pre
    )
    return head_grad, gate_grad, up_grad


def solution(mesh):
    in_specs = (
        P("wide", "narrow"),
        P("wide", "narrow"),
        P(),
        P(),
        P(),
        P(None, "wide", None),
        P(None, "wide"),
        P("wide", "narrow"),
        P("wide", "narrow"),
        P("narrow", None),
    )
    out_specs = (P("wide", "narrow"), P("wide", "narrow"), P("wide", "narrow"))

    return jax.shard_map(
        on_device, mesh=mesh, in_specs=in_specs, out_specs=out_specs, check_vma=False
    )
```
